256 devices in a mesh: tiles: 32 (over z, x), sub: 8 (over y, core).
Axes of the slice: x: 4, y: 4, z: 8, core: 2. Of those that a mesh axis runs over, the one named last changes fastest.
Arguments:
- latents: float32 [196608, 512], P(('tiles', 'sub')), may hold values from -130 to 130
- conv_weight: float32 [512, 9, 512], P('tiles'), may hold values from -0.09375 to 0.09375
- conv_bias: float32 [512], replicated, may hold values from -4 to 4
- norm1_gain: float32 [512], replicated, may hold values from 0.5 to 1.5
- norm1_shift: float32 [512], replicated, may hold values from -3 to 3
- norm2_gain: float32 [512], replicated, may hold values from 0.5 to 1.5
- norm2_shift: float32 [512], replicated, may hold values from -3 to 3
- tile_counts: int32 [36], replicated, may hold values from 1 to 64, 768 in all
- widths: int32 [36], replicated, may hold values from 32 to 128, as said below
Outputs:
- activated: float32 [196608, 512], P(('tiles', 'sub'))
The draws below stay inside these ranges and needn't reach their ends.
Inputs may be any that keep to these rules, and one draw needn't show every extreme that they name: `widths`: each width is 128, 64 or 32; some image has width 128 and some has width 128 / 4. `tile_counts`: they add up to 768; the largest is 64.
All inputs are finite; a program needn't handle non-finite values.
Results may differ from the reference program's by a relative error of at most 0.00014.
Values sent between devices are 32-bit elements; how exact they have to be, the bound alone decides.
A program may use at most 128 MiB of HBM per device.

```python
import math
import jax
import jax.numpy as jnp
import numpy as np
from jax import lax

C = 512
GROUPS = 32
WMAX = 128
TILE = 256
TOTAL_TILES = 768
MOST_TILES = 64
PIX_DEV = 768
PIXELS = 196608
IMAGES = 36


def draw_latents(key, part):
    subkeys = jax.random.split(jax.random.fold_in(key, 7), 4)
    position = jnp.arange(PIXELS, dtype=jnp.float32) / PIXELS
    upward_trend = jnp.exp(position * math.log(3.0))[:, None]
    row_scale = jnp.exp(jax.random.uniform(subkeys[1], (PIXELS, 1)) * math.log(10.0)) * upward_trend
    column_scale = jnp.exp(jax.random.uniform(subkeys[2], (1, C)) * math.log(10.0))
    offsets = jax.random.uniform(subkeys[3], (1, C), minval=-1.0, maxval=1.0)
    normal_part = jax.random.truncated_normal(subkeys[0], -4.0, 4.0, (PIXELS, C))
    values = normal_part * row_scale * column_scale / 10.0 + offsets
    return values.astype(jnp.float32)


def draw_widths(key, part):
    subkeys = jax.random.split(jax.random.fold_in(key, 13), 3)
    halvings = jax.random.randint(subkeys[0], (IMAGES,), 0, 3).astype(jnp.int32)
    values = jnp.right_shift(jnp.full((IMAGES,), WMAX, jnp.int32), halvings)
    widest = jax.random.randint(subkeys[1], (), 0, IMAGES)
    narrowest = (widest + 1 + jax.random.randint(subkeys[2], (), 0, IMAGES - 1)) % IMAGES
    image_index = jnp.arange(IMAGES)
    values = jnp.where(image_index == widest, WMAX, values)
    values = jnp.where(image_index == narrowest, WMAX // 4, values)
    return values.astype(jnp.int32)


def level_of(stream_key, shape, shards, smallest, top_value):
    def one(dim, blocks):
        heights = jax.random.uniform(jax.random.fold_in(jax.random.fold_in(stream_key, 6), dim), (blocks,), jnp.float32, smallest / len(shards), top_value / len(shards))
        return jnp.repeat(jnp.exp(heights), shape[dim] // blocks).reshape((-1,) + (1,) * (len(shape) - dim - 1))

    gain = one(*shards[0])
    for cut in shards[1:]:
        gain = gain * one(*cut)
    return gain


def split_up(number_of, total, limit, slope):
    loads = [(1 << 20) // math.isqrt(grade ** slope) + 1 for grade in range(2, number_of + 1)]
    surplus, given = total - limit - (number_of - 1), [1] * (number_of - 1)
    while surplus > 0:
        free = [i for i in range(number_of - 1) if given[i] < limit]
        mass, budget = sum([loads[i] for i in free]), surplus
        for i in free:
            more = min(limit - given[i], max(1, budget * loads[i] // mass), surplus)
            given[i] = given[i] + more
            surplus = surplus - more
    return np.array([limit] + given)


def uneven(key, amount, total, limit, lean):
    if amount == 2:
        one = jax.random.randint(key, (), max(1, total - limit), min(limit, total - 1) + 1)
        return jnp.stack([one, total - one])
    tallies = jnp.asarray(split_up(amount, total, limit, lean), jnp.int32)
    couples = (amount - 1) // 2
    giver, receiver = tallies[1:1 + 2 * couples:2], tallies[2:2 + 2 * couples:2]
    room = jnp.minimum(giver - 1, limit - receiver)
    shifted = jax.random.randint(jax.random.fold_in(key, 1), (couples,), 0, 1 << 20) % (room + 1)
    tallies = tallies.at[1:1 + 2 * couples:2].set(giver - shifted).at[2:2 + 2 * couples:2].set(receiver + shifted)
    return tallies[jax.random.permutation(jax.random.fold_in(key, 2), amount)]


def normal_values(key, shape, scale, bound, cuts=(), kind=jnp.bfloat16):
    values = jax.random.normal(key, shape, jnp.float32) * scale
    if len(cuts) > 0:
        values = level_of(key, shape, cuts, -0.22, 0.18) * values
    return jnp.clip(values, min=-bound, max=bound).astype(kind)


def setup_inputs(seed: int = 0) -> dict:
    seeds = jax.random.split(jax.random.key(seed), 10)
    return {
        "latents": draw_latents(jax.random.fold_in(seeds[9], 71), 0),
        "conv_weight": normal_values(seeds[1], (C, 9, C), (9 * C) ** -0.5, 0.09375, ((0, 32),), jnp.float32),
        "conv_bias": normal_values(seeds[2], (C,), 1.0, 4.0, (), jnp.float32),
        "norm1_gain": jnp.clip(jax.random.uniform(seeds[3], (C,), jnp.float32, 0.5, 1.5), 0.5, 1.5),
        "norm1_shift": normal_values(seeds[4], (C,), 0.5, 3.0, (), jnp.float32),
        "norm2_gain": jnp.clip(jax.random.uniform(seeds[5], (C,), jnp.float32, 0.5, 1.5), 0.5, 1.5),
        "norm2_shift": normal_values(seeds[6], (C,), 0.5, 3.0, (), jnp.float32),
        "tile_counts": uneven(seeds[7], IMAGES, TOTAL_TILES, MOST_TILES, 2).astype(jnp.int32),
        "widths": draw_widths(jax.random.fold_in(seeds[9], 71), 0),
    }


epsilon = 1e-06

def layout(tile_counts, widths):
    pixel_counts = (tile_counts * TILE).astype(jnp.int32)
    image_ends = jnp.cumsum(pixel_counts).astype(jnp.int32)
    image_starts = image_ends - pixel_counts
    position = jnp.arange(PIXELS, dtype=jnp.int32)
    image_id = lax.optimization_barrier(jnp.sum((position[:, None] >= image_ends[None, :]).astype(jnp.int32), axis=1)).astype(jnp.int32)
    pixel_width = widths[image_id]
    offset = position - image_starts[image_id]
    row_index = offset // pixel_width
    column_index = offset - row_index * pixel_width
    pixel_height = pixel_counts[image_id] // pixel_width
    return (image_id, pixel_counts, row_index, column_index, pixel_width, pixel_height)

def group_norm(values, norm_gain, norm_shift, image_id, pixel_counts):
    group_size = C // GROUPS
    entries = (pixel_counts * group_size).astype(jnp.float32)[:, None]
    firsts = jax.ops.segment_sum(values, image_id, num_segments=IMAGES)
    group_mean = lax.optimization_barrier(jnp.sum(firsts.reshape(IMAGES, GROUPS, group_size), axis=2)) / entries
    centred = values - jnp.repeat(group_mean, group_size, axis=1)[image_id]
    squares = jax.ops.segment_sum(centred * centred, image_id, num_segments=IMAGES)
    spread = lax.optimization_barrier(jnp.sum(squares.reshape(IMAGES, GROUPS, group_size), axis=2)) / entries
    inverse = jnp.repeat(lax.rsqrt(spread + epsilon), group_size, axis=1)[image_id]
    return jax.nn.silu(centred * inverse * norm_gain + norm_shift)

def tap_tables(row_index, column_index, pixel_width, pixel_height):
    anchor = jnp.arange(PIXELS, dtype=jnp.int32) + (WMAX + 1)
    sources = []
    validity = []
    for step_y in (-1, 0, 1):
        for step_x in (-1, 0, 1):
            inside = (row_index + step_y >= 0) & (row_index + step_y < pixel_height)
            inside = inside & (column_index + step_x >= 0) & (column_index + step_x < pixel_width)
            sources.append(jnp.where(inside, anchor + step_y * pixel_width + step_x, anchor).astype(jnp.int32))
            validity.append(inside.astype(jnp.float32))
    return (jnp.stack(sources), jnp.stack(validity))

def convolve(activated, conv_weight, conv_bias, sources, validity):
    padded = jnp.pad(activated, ((WMAX + 1, WMAX + 1), (0, 0)))
    block_count = PIXELS // PIX_DEV
    source_blocks = sources.reshape(9, block_count, PIX_DEV).transpose(1, 0, 2)
    mask_blocks = validity.reshape(9, block_count, PIX_DEV).transpose(1, 0, 2)

    def one_block(block_pair):
        block_sources, block_masks = block_pair
        running = jnp.zeros((PIX_DEV, C), jnp.float32)
        for tap_index in range(9):
            gathered = padded[block_sources[tap_index]] * block_masks[tap_index][:, None]
            running = running + jnp.dot(gathered, conv_weight[:, tap_index, :], precision=lax.Precision.HIGHEST, preferred_element_type=jnp.float32)
        return running
    result = lax.map(one_block, (source_blocks, mask_blocks)).reshape(PIXELS, C)
    return result + conv_bias

def reference(latents, conv_weight, conv_bias, norm1_gain, norm1_shift, norm2_gain, norm2_shift, tile_counts, widths):
    image_id, pixel_counts, row_index, column_index, pixel_width, pixel_height = layout(tile_counts, widths)
    first_act = group_norm(latents, norm1_gain, norm1_shift, image_id, pixel_counts)
    sources, validity = tap_tables(row_index, column_index, pixel_width, pixel_height)
    hidden = convolve(first_act, conv_weight, conv_bias, sources, validity)
    return group_norm(hidden, norm2_gain, norm2_shift, image_id, pixel_counts)
```

```python
import functools

import jax
import jax.numpy as jnp
from jax import lax
from jax.experimental import pallas as pl
from jax.experimental.pallas import tpu as pltpu
from jax.sharding import PartitionSpec as P

MESH = pl.DeviceIdType.MESH
F32 = jnp.float32
BF16 = jnp.bfloat16

TILE = 256
GROUP = 16
HALF = 128
EPS = 1e-06
WINDOW = 21
PEERS = 2 * WINDOW
A_TAPS = (0, 4)
B_TAPS = (4, 5)
FULL, LOW, HIGH = 0, 1, 2


def lane_iota(shape):
    return lax.broadcasted_iota(jnp.int32, shape, len(shape) - 1)


def butterfly(values, step):
    lanes = lane_iota(values.shape)
    up = pltpu.roll(values, step, 1)
    down = pltpu.roll(values, HALF - step, 1)
    return values + jnp.where((lanes & step) != 0, up, down)


def fold_lanes(rows):
    return jnp.concatenate([rows[:, HALF * b : HALF * (b + 1)] for b in range(4)], axis=0)


def unfold_lanes(folded):
    return jnp.concatenate([folded[8 * b : 8 * (b + 1)] for b in range(4)], axis=1)


def group_sum(rows):
    folded = fold_lanes(rows)
    for step in (1, 2, 4, 8):
        folded = butterfly(folded, step)
    return folded


def pack_groups(folded):
    lanes = lane_iota((8, HALF))
    packed = jnp.zeros((8, HALF), F32)
    for b in range(4):
        packed = jnp.where((lanes & 3) == b, folded[8 * b : 8 * (b + 1)], packed)
    return packed


def unpack_groups(packed):
    lanes = lane_iota((8, HALF))
    blocks = []
    for b in range(4):
        block = jnp.where((lanes & 3) == b, packed, 0.0)
        block = butterfly(butterfly(block, 1), 2)
        blocks.append(block)
    return jnp.concatenate(blocks, axis=1)


def rows_of(parts):
    zeros = jnp.zeros((8 - len(parts), parts[0].shape[1]), F32)
    return jnp.concatenate(parts + [zeros], axis=0)


def tile_stats(ref):
    sums = rows_of(
        [jnp.sum(ref[TILE * j : TILE * (j + 1), :], axis=0, keepdims=True) for j in range(3)]
    )
    total = group_sum(sums)
    means = unfold_lanes(total * (1.0 / (TILE * GROUP)))
    seconds = []
    for j in range(3):
        off = ref[TILE * j : TILE * (j + 1), :] - means[j : j + 1]
        seconds.append(jnp.sum(off * off, axis=0, keepdims=True))
    spread = group_sum(rows_of(seconds))
    return pack_groups(total) + pltpu.roll(pack_groups(spread), 4, 0)


def image_stats(win, stat, me, starts, ends):
    rows = win.shape[0] + 8
    table = jnp.concatenate([win[...], stat[...]], axis=0)
    row = lax.broadcasted_iota(jnp.int32, (rows, HALF), 0)
    slot = row >> 3
    tile_row = row & 7
    offset = jnp.where(slot >= WINDOW, slot - WINDOW + 1, slot - WINDOW)
    offset = jnp.where(slot >= PEERS, 0, offset)
    tile = 3 * (me + offset) + tile_row
    second = pltpu.roll(table.reshape(rows // 8, 8, HALF), 4, 1).reshape(rows, HALF)
    tile_mean = table * (1.0 / (TILE * GROUP))
    means, inverses = [], []
    for j in range(3):
        member = (tile >= starts[j]) & (tile < ends[j]) & (tile_row < 3)
        count = jnp.full((1, HALF), (ends[j] - starts[j]) * (TILE * GROUP), jnp.int32).astype(F32)
        mean = jnp.sum(jnp.where(member, table, 0.0), axis=0, keepdims=True) / count
        away = tile_mean - mean
        moment = second + (TILE * GROUP) * (away * away)
        spread = jnp.sum(jnp.where(member, moment, 0.0), axis=0, keepdims=True) / count
        means.append(mean)
        inverses.append(lax.rsqrt(spread + EPS))
    packed = rows_of(means) + pltpu.roll(rows_of(inverses), 4, 0)
    return unpack_groups(packed)


def kernel(
    counts,
    widths,
    latents,
    weight,
    bias,
    gain,
    shift,
    hidden,
    coef_out,
    local,
    halo,
    taps_a,
    taps_b,
    acts,
    total,
    w_high,
    w_low,
    coef,
    stat1,
    stat2,
    win1,
    win2,
    local_sem,
    halo_send,
    halo_recv,
    stat_send,
    stat_recv,
    send_sem,
    ax_recv,
    az_recv,
    bz_recv,
    bx_recv,
    pair_recv,
):
    t = lax.axis_index("tiles")
    s = lax.axis_index("sub")
    me = t * 8 + s
    z, x = t // 4, t % 4
    core = s % 2

    def at(index):
        p = lax.rem(index + 256, 256)
        return (p // 8, p % 8)

    right = {
        "z+": (lax.rem(z + 1, 8) * 4 + x, s),
        "z-": (lax.rem(z + 7, 8) * 4 + x, s),
        "x+": (z * 4 + lax.rem(x + 1, 4), s),
        "x-": (z * 4 + lax.rem(x + 3, 4), s),
        "c": (t, s + 1 - 2 * core),
    }

    def z_row(dz):
        return lax.rem(z + dz + 8, 8) * 4

    def row_of(dz, dx):
        return z_row(dz) + lax.rem(x + dx + 4, 4)

    barrier = pltpu.get_barrier_semaphore()

    def greet(step, carry):
        for sign in (1, -1):
            pl.semaphore_signal(barrier, inc=1, device_id=at(me + sign * step), device_id_type=MESH)
        return carry

    for name in ("z+", "z-", "x+", "x-"):
        pl.semaphore_signal(barrier, inc=1, device_id=right[name], device_id_type=MESH)
    lax.fori_loop(1, WINDOW + 1, greet, 0)

    load = pltpu.make_async_copy(latents, local, local_sem.at[0])
    load.start()

    own = [
        pltpu.make_async_copy(weight.at[pl.ds(0, 4)], taps_a.at[t], local_sem.at[1]),
        pltpu.make_async_copy(weight.at[pl.ds(4, 5)], taps_b.at[t], local_sem.at[1]),
    ]
    for owner in range(2):
        pl.when(core == owner)(own[owner].start)

    tiles = [3 * me + j for j in range(3)]
    starts = [me * 0] * 3
    ends = [me * 0] * 3
    width = [me * 0 + 32] * 3
    begin = me * 0

    def place(i, carry):
        begin, starts, ends, width = carry
        end = begin + counts[i]
        inside = [(tile >= begin) & (tile < end) for tile in tiles]
        starts = [jnp.where(hit, begin, old) for hit, old in zip(inside, starts)]
        ends = [jnp.where(hit, end, old) for hit, old in zip(inside, ends)]
        width = [jnp.where(hit, widths[i], old) for hit, old in zip(inside, width)]
        return end, starts, ends, width

    _, starts, ends, width = lax.fori_loop(
        0, counts.shape[0], place, (begin, starts, ends, width)
    )

    def piece(taps, first, count):
        if taps[0] < 4:
            return taps_a.at[pl.ds(first, count), pl.ds(taps[0], taps[1])]
        return taps_b.at[pl.ds(first, count), pl.ds(taps[0] - 4, taps[1])]

    sent = {0: [], 1: []}

    def send(owner, taps, first, count, way, recv):
        ref = piece(taps, first, count)
        copy = pltpu.make_async_remote_copy(
            src_ref=ref,
            dst_ref=ref,
            send_sem=send_sem.at[len(sent[owner])],
            recv_sem=recv,
            device_id=right[way],
            device_id_type=MESH,
        )
        copy.start()
        sent[owner].append((taps, count))

    def arrived(taps, first, count, recv):
        ref = piece(taps, first, count)
        pltpu.make_async_remote_copy(
            src_ref=ref,
            dst_ref=ref,
            send_sem=send_sem.at[0],
            recv_sem=recv,
            device_id=right["c"],
            device_id_type=MESH,
        ).wait_recv()

    group_of = {0: 0, -1: 1, 1: 2, -2: 3, 2: 4, -3: 5, 3: 6, 4: 7}
    a_low, a_high = (0, 2), (2, 2)
    b_low, b_high = (4, 2), (6, 3)

    def a_start():
        own[0].wait()
        send(0, A_TAPS, row_of(0, 0), 1, "x+", ax_recv.at[0])
        send(0, A_TAPS, row_of(0, 0), 1, "x-", ax_recv.at[1])

    def a_x_near():
        arrived(A_TAPS, row_of(0, -1), 1, ax_recv.at[0])
        send(0, a_low, row_of(0, -1), 1, "x+", ax_recv.at[2])
        arrived(A_TAPS, row_of(0, 1), 1, ax_recv.at[1])
        send(0, a_high, row_of(0, 1), 1, "x-", ax_recv.at[3])

    def a_x_far():
        arrived(a_low, row_of(0, 2), 1, ax_recv.at[2])
        arrived(a_high, row_of(0, 2), 1, ax_recv.at[3])
        for h in range(2):
            send(0, A_TAPS, z_row(0) + 2 * h, 2, "z+", az_recv.at[h])
            send(0, A_TAPS, z_row(0) + 2 * h, 2, "z-", az_recv.at[6 + h])
        send(0, A_TAPS, z_row(0), 4, "c", pair_recv.at[0])

    def a_z(d):
        if d == 4:
            arrived(A_TAPS, z_row(4), 2, az_recv.at[12])
            arrived(A_TAPS, z_row(4) + 2, 2, az_recv.at[13])
            send(0, A_TAPS, z_row(4), 4, "c", pair_recv.at[7])
            return
        for h in range(2):
            for way in range(2):
                dz = d if way else -d
                row = z_row(dz) + 2 * h
                arrived(A_TAPS, row, 2, az_recv.at[way * 6 + (d - 1) * 2 + h])
                if d < 3:
                    send(0, A_TAPS, row, 2, "z-" if way else "z+", az_recv.at[way * 6 + d * 2 + h])
                elif way == h:
                    send(0, A_TAPS, row, 2, "z-" if way else "z+", az_recv.at[12 + h])
        for dz in (-d, d):
            send(0, A_TAPS, z_row(dz), 4, "c", pair_recv.at[group_of[dz]])

    def b_spread(dz):
        g = group_of[dz]
        send(1, B_TAPS, row_of(dz, 0), 1, "x+", bx_recv.at[4 * g])
        send(1, B_TAPS, row_of(dz, 0), 1, "x-", bx_recv.at[4 * g + 1])

    def b_start():
        own[1].wait()
        send(1, B_TAPS, row_of(0, 0), 1, "z+", bz_recv.at[0])
        send(1, B_TAPS, row_of(0, 0), 1, "z-", bz_recv.at[3])
        b_spread(0)

    def b_z(d):
        if d == 4:
            arrived(b_low, row_of(4, 0), 1, bz_recv.at[6])
            arrived(b_high, row_of(4, 0), 1, bz_recv.at[7])
            b_spread(4)
            return
        for way in range(2):
            dz = d if way else -d
            arrived(B_TAPS, row_of(dz, 0), 1, bz_recv.at[way * 3 + d - 1])
            if d < 3:
                send(1, B_TAPS, row_of(dz, 0), 1, "z-" if way else "z+", bz_recv.at[way * 3 + d])
            else:
                taps = b_high if way else b_low
                send(1, taps, row_of(dz, 0), 1, "z-" if way else "z+", bz_recv.at[6 + way])
            b_spread(dz)

    def b_near(dz):
        g = group_of[dz]
        arrived(B_TAPS, row_of(dz, -1), 1, bx_recv.at[4 * g])
        send(1, b_low, row_of(dz, -1), 1, "x+", bx_recv.at[4 * g + 2])
        arrived(B_TAPS, row_of(dz, 1), 1, bx_recv.at[4 * g + 1])
        send(1, b_high, row_of(dz, 1), 1, "x-", bx_recv.at[4 * g + 3])

    def b_far(dz):
        g = group_of[dz]
        arrived(b_low, row_of(dz, 2), 1, bx_recv.at[4 * g + 2])
        arrived(b_high, row_of(dz, 2), 1, bx_recv.at[4 * g + 3])
        send(1, B_TAPS, z_row(dz), 4, "c", pair_recv.at[g])

    def serve(a_steps, b_steps):
        @pl.when(core == 0)
        def _():
            for step in a_steps:
                step()

        @pl.when(core == 1)
        def _():
            for step in b_steps:
                step()

    def pair_arrived(groups):
        @pl.when(core == 0)
        def _():
            for dz in groups:
                arrived(B_TAPS, z_row(dz), 4, pair_recv.at[group_of[dz]])

        @pl.when(core == 1)
        def _():
            for dz in groups:
                arrived(A_TAPS, z_row(dz), 4, pair_recv.at[group_of[dz]])

    do = functools.partial

    load.wait()
    stat1[...] = tile_stats(local)
    for h in range(8):
        rows = pl.ds(96 * h, 96)
        total[rows, :] = jnp.broadcast_to(bias[...], (96, 512))

    pl.semaphore_wait(barrier, PEERS + 4)
    serve([a_start], [b_start])
    up = pltpu.make_async_remote_copy(
        src_ref=latents.at[pl.ds(5 * HALF, HALF), :],
        dst_ref=halo.at[0],
        send_sem=halo_send.at[0],
        recv_sem=halo_recv.at[0],
        device_id=at(me + 1),
        device_id_type=MESH,
    )
    down = pltpu.make_async_remote_copy(
        src_ref=latents.at[pl.ds(0, HALF), :],
        dst_ref=halo.at[1],
        send_sem=halo_send.at[1],
        recv_sem=halo_recv.at[1],
        device_id=at(me - 1),
        device_id_type=MESH,
    )

    def share(stat, win, which):
        def one(step, carry):
            for slot, to in ((WINDOW - step, me + step), (WINDOW - 1 + step, me - step)):
                pltpu.make_async_remote_copy(
                    src_ref=stat,
                    dst_ref=win.at[pl.ds(pl.multiple_of(slot * 8, 8), 8), :],
                    send_sem=stat_send.at[which],
                    recv_sem=stat_recv.at[which],
                    device_id=at(to),
                    device_id_type=MESH,
                ).start()
            return carry

        lax.fori_loop(1, WINDOW + 1, one, 0)

    def collect(win, which):
        ref = win
        both = pltpu.make_async_remote_copy(
            src_ref=ref,
            dst_ref=ref,
            send_sem=stat_send.at[which],
            recv_sem=stat_recv.at[which],
            device_id=at(me + 1),
            device_id_type=MESH,
        )
        both.wait_send()
        both.wait_recv()

    share(stat1, win1, 0)
    up.start()
    down.start()
    serve([a_x_near], [do(b_z, 1), do(b_near, 0)])
    serve([a_x_far], [do(b_z, 2), do(b_far, 0), do(b_near, -1), do(b_near, 1)])
    collect(win1, 0)
    coef[...] = image_stats(win1, stat1, me, starts, ends)
    up.wait()
    down.wait()

    def act_block(source, j, wide, stores):
        row = lax.broadcasted_iota(jnp.int32, (HALF, HALF), 0)
        column = row & (wide - 1)
        has_left = column != 0
        has_right = column != wide - 1
        for b in range(4):
            lanes = pl.ds(HALF * b, HALF)
            mean = coef[pl.ds(j, 1), lanes]
            scale = coef[pl.ds(j + 4, 1), lanes] * gain[:, HALF * b : HALF * (b + 1)]
            value = (source(lanes) - mean) * scale + shift[:, HALF * b : HALF * (b + 1)]
            act = value / (1.0 + jnp.exp(-value))
            shifted = (
                jnp.where(has_left, pltpu.roll(act, 1, 0), 0.0),
                act,
                jnp.where(has_right, pltpu.roll(act, HALF - 1, 0), 0.0),
            )
            for dx in range(3):
                high = shifted[dx].astype(BF16)
                low = (shifted[dx] - high.astype(F32)).astype(BF16)
                for base, valid in stores:
                    rows = pl.ds(base, HALF)
                    if valid is None:
                        acts[dx, 0, rows, lanes] = high
                        acts[dx, 1, rows, lanes] = low
                    else:
                        keep = jnp.where(valid, 1.0, 0.0).astype(F32)
                        acts[dx, 0, rows, lanes] = (high.astype(F32) * keep).astype(BF16)
                        acts[dx, 1, rows, lanes] = (low.astype(F32) * keep).astype(BF16)

    act_block(lambda lanes: halo[0, :, lanes], 0, width[0], [(0, tiles[0] > starts[0])])
    act_block(lambda lanes: halo[1, :, lanes], 2, width[2], [(2 * 512 + 384, tiles[2] + 1 < ends[2])])
    for q in range(6):
        j, half = q // 2, q % 2
        stores = [(j * 512 + HALF + half * HALF, None)]
        if half == 0 and j > 0:
            stores.append(((j - 1) * 512 + 384, tiles[j] > starts[j]))
        if half == 1 and j < 2:
            stores.append(((j + 1) * 512, tiles[j + 1] > starts[j + 1]))
        act_block(lambda lanes, q=q: local[HALF * q : HALF * (q + 1), lanes], j, width[j], stores)

    serve(
        [do(a_z, 1)],
        [do(b_z, 3), do(b_far, -1), do(b_far, 1), do(b_near, -2), do(b_near, 2)],
    )

    odd = z % 2
    first = z // 2
    order = [
        first,
        lax.rem(first + 3 + 2 * odd, 4),
        lax.rem(first + 1 + 2 * odd, 4),
        lax.rem(first + 2, 4),
    ]
    groups = [(0, -1, 1), (-2, 2), (-3, 3), (4,)]

    def split_weights(chunk):
        def fixed(c):
            for source, skip in ((taps_a, 0), (taps_b, 4)):
                for tap in range(source.shape[1]):
                    value = source[8 * c : 8 * c + 8, tap : tap + 1].reshape(HALF, 512)
                    to = pl.ds((tap + skip) * HALF, HALF)
                    high = value.astype(BF16)
                    w_high[to, :] = high
                    w_low[to, :] = (value - high.astype(F32)).astype(BF16)

        for c in range(4):
            pl.when(chunk == c)(functools.partial(fixed, c))

    def multiply(chunk, j):
        lanes = pl.ds(pl.multiple_of(chunk * HALF, HALF), HALF)
        wide = width[j]

        is_wide, is_middle = wide == 128, wide == 64

        def taps(part):
            columns = []
            for dy in (-1, 0, 1):
                for dx in range(3):
                    base = j * 512 + HALF
                    if dy == 0:
                        columns.append(acts[dx, part, pl.ds(base, TILE), lanes])
                        continue
                    near = acts[dx, part, pl.ds(base + 32 * dy, TILE), lanes]
                    middle = acts[dx, part, pl.ds(base + 64 * dy, TILE), lanes]
                    far = acts[dx, part, pl.ds(base + 128 * dy, TILE), lanes]
                    columns.append(
                        jnp.where(is_wide, far, jnp.where(is_middle, middle, near))
                    )
            return jnp.concatenate(columns, axis=1)

        high = taps(0)
        low = taps(1)
        out = jnp.dot(high, w_high[...], preferred_element_type=F32)
        out += jnp.dot(low, w_high[...], preferred_element_type=F32)
        out += jnp.dot(high, w_low[...], preferred_element_type=F32)
        rows = pl.ds(pl.multiple_of(j * TILE, TILE), TILE)
        total[rows, :] += out

    between = {
        (0, 0): ([], [do(b_z, 4)]),
        (0, 1): ([], [do(b_far, -2), do(b_far, 2)]),
        (0, 2): ([do(a_z, 2)], [do(b_near, -3), do(b_near, 3)]),
        (1, 0): ([], [do(b_far, -3), do(b_far, 3)]),
        (1, 1): ([], [do(b_near, 4)]),
        (1, 2): ([do(a_z, 3)], [do(b_far, 4)]),
        (2, 2): ([do(a_z, 4)], []),
    }

    for k in range(4):
        pair_arrived(groups[k])
        split_weights(order[k])
        for j in range(3):
            multiply(order[k], j)
            if (k, j) in between:
                serve(*between[(k, j)])

    store = pltpu.make_async_copy(total, hidden, local_sem.at[6])
    store.start()
    stat2[...] = tile_stats(total)
    share(stat2, win2, 1)
    for owner in range(2):

        @pl.when(core == owner)
        def _(owner=owner):
            for index, (taps, count) in enumerate(sent[owner]):
                ref = piece(taps, z_row(0), count)
                pltpu.make_async_remote_copy(
                    src_ref=ref,
                    dst_ref=ref,
                    send_sem=send_sem.at[index],
                    recv_sem=pair_recv.at[0],
                    device_id=right["c"],
                    device_id_type=MESH,
                ).wait_send()

    collect(win2, 1)
    coef_out[...] = image_stats(win2, stat2, me, starts, ends)
    store.wait()


def shards(latents, weight, bias, gain1, shift1, gain2, shift2, tile_counts, widths):
    vmem = pl.BlockSpec(memory_space=pltpu.VMEM)
    smem = pl.BlockSpec(memory_space=pltpu.SMEM)
    hbm = pl.BlockSpec(memory_space=pl.ANY)
    dma = pltpu.SemaphoreType.DMA
    pixels, channels = latents.shape
    hidden, coef = pl.pallas_call(
        kernel,
        out_shape=(
            jax.ShapeDtypeStruct((pixels, channels), F32),
            jax.ShapeDtypeStruct((8, channels), F32),
        ),
        in_specs=[smem, smem, hbm, hbm, vmem, vmem, vmem],
        out_specs=(hbm, vmem),
        scratch_shapes=[
            pltpu.VMEM((pixels, channels), F32),
            pltpu.VMEM((2, HALF, channels), F32),
            pltpu.VMEM((32, 4, 16, channels), F32),
            pltpu.VMEM((32, 5, 16, channels), F32),
            pltpu.VMEM((3, 2, 1536, channels), BF16),
            pltpu.VMEM((pixels, channels), F32),
            pltpu.VMEM((9 * HALF, channels), BF16),
            pltpu.VMEM((9 * HALF, channels), BF16),
            pltpu.VMEM((8, channels), F32),
            pltpu.VMEM((8, HALF), F32),
            pltpu.VMEM((8, HALF), F32),
            pltpu.VMEM((8 * PEERS, HALF), F32),
            pltpu.VMEM((8 * PEERS, HALF), F32),
            dma((7,)),
            dma((2,)),
            dma((2,)),
            dma((2,)),
            dma((2,)),
            dma((48,)),
            dma((4,)),
            dma((14,)),
            dma((8,)),
            dma((32,)),
            dma((8,)),
        ],
        compiler_params=pltpu.CompilerParams(
            collective_id=0, has_side_effects=True, vmem_limit_bytes=60 << 20
        ),
        name="block",
    )(
        tile_counts,
        widths,
        latents,
        jnp.transpose(weight, (1, 0, 2)),
        bias.reshape(1, -1),
        gain1.reshape(1, -1),
        shift1.reshape(1, -1),
    )
    centred = hidden.reshape(3, TILE, channels) - coef[0:3, None, :]
    value = centred * (coef[4:7, None, :] * gain2) + shift2
    return jax.nn.silu(value).reshape(pixels, channels)


def solution(mesh):
    return jax.shard_map(
        shards,
        mesh=mesh,
        in_specs=(
            P(("tiles", "sub"), None),
            P("tiles", None, None),
            P(),
            P(),
            P(),
            P(),
            P(),
            P(),
            P(),
        ),
        out_specs=P(("tiles", "sub"), None),
        check_vma=False,
    )
```

```python
import functools

import jax
import jax.numpy as jnp
from jax import lax
from jax.experimental import pallas as pl
from jax.experimental.pallas import tpu as pltpu
from jax.sharding import PartitionSpec as P

MESH = pl.DeviceIdType.MESH
F32 = jnp.float32
BF16 = jnp.bfloat16

TILE = 256
GROUP = 16
HALF = 128
EPS = 1e-06
WINDOW = 21
PEERS = 2 * WINDOW


START = ([("a_start",)], [("b_start",)])
SERVE = {
    "stats": (
        [("a_near", "y"), ("a_near", "a"), ("a_far", "y")],
        [("b_z", 1, 0), ("b_z", 1, 1)],
    ),
    "act0": (
        [("a_far", "a")],
        [("b_near", 0)],
    ),
    "act6": (
        [("y_near", 0, 0), ("y_near", 0, 1)],
        [("b_z", 2, 0), ("b_z", 2, 1)],
    ),
    "act7": (
        [("a_z", "y", 1, 0, 0), ("a_z", "y", 1, 1, 0)],
        [],
    ),
    "pre00": (
        [("a_z", "y", 1, 0, 1), ("a_z", "y", 1, 1, 1), ("a_done", "y", 1), ("a_done", "y", -1), ("a_z", "a", 1, 0, 0), ("a_z", "a", 1, 1, 0), ("a_z", "a", 1, 0, 1), ("a_z", "a", 1, 1, 1), ("a_done", "a", 1), ("a_done", "a", -1), ("y_far", 0), ("a_z", "y", 2, 0, 0), ("a_z", "y", 2, 1, 0), ("y_near", 1, 0), ("y_near", 1, 1), ("a_z", "y", 2, 0, 1), ("a_z", "y", 2, 1, 1), ("a_done", "y", -2), ("a_done", "y", 2), ("a_z", "a", 2, 0, 0), ("a_z", "a", 2, 1, 0), ("y_near", -1, 0), ("y_near", -1, 1), ("a_z", "a", 2, 0, 1), ("a_z", "a", 2, 1, 1), ("a_done", "a", -2), ("a_done", "a", 2), ("y_far", 1), ("a_z", "y", 3, 0, 0), ("a_z", "y", 3, 1, 0)],
        [("b_near", -1), ("b_near", 1), ("b_far", 0), ("b_z", 3, 0), ("b_z", 3, 1), ("b_near", -2), ("b_near", 2), ("b_far", -1), ("b_far", 1), ("b_last",)],
    ),
    "post000": (
        [("a_z", "y", 3, 0, 1), ("a_z", "y", 3, 1, 1), ("a_done", "y", 3), ("a_done", "y", -3), ("y_near", -2, 0), ("y_near", -2, 1)],
        [],
    ),
    "post001": (
        [("a_z", "a", 3, 0, 0), ("a_z", "a", 3, 1, 0)],
        [("b_near", 3), ("b_near", -3)],
    ),
    "post002": (
        [("a_z", "a", 3, 0, 1), ("a_z", "a", 3, 1, 1), ("a_done", "a", 3), ("a_done", "a", -3), ("y_near", 2, 0), ("y_near", 2, 1)],
        [("b_far", -2), ("b_far", 2)],
    ),
    "post010": (
        [("a_z", "y", 4, 0, 0), ("y_far", -1)],
        [],
    ),
    "post011": (
        [("a_z", "y", 4, 0, 1), ("a_done", "y", 4)],
        [("b_near", 4)],
    ),
    "post012": (
        [("a_z", "a", 4, 0, 0), ("y_near", 3, 0), ("y_near", 3, 1)],
        [],
    ),
    "post100": (
        [("a_z", "a", 4, 0, 1), ("a_done", "a", 4)],
        [("b_far", 3), ("b_far", -3)],
    ),
    "post101": (
        [("y_near", -3, 0), ("y_near", -3, 1)],
        [],
    ),
    "post102": (
        [("y_far", -2)],
        [("b_far", 4)],
    ),
    "pre11": (
        [("y_far", 2)],
        [],
    ),
    "post110": (
        [("y_near", 4, 0), ("y_near", 4, 1)],
        [],
    ),
    "post111": (
        [("y_far", 3)],
        [],
    ),
    "post112": (
        [("y_far", -3)],
        [],
    ),
    "post201": (
        [("y_far", 4)],
        [],
    ),
}


def lane_iota(shape):
    return lax.broadcasted_iota(jnp.int32, shape, len(shape) - 1)


def butterfly(values, step):
    lanes = lane_iota(values.shape)
    up = pltpu.roll(values, step, 1)
    down = pltpu.roll(values, HALF - step, 1)
    return values + jnp.where((lanes & step) != 0, up, down)


def fold_lanes(rows):
    return jnp.concatenate([rows[:, HALF * b : HALF * (b + 1)] for b in range(4)], axis=0)


def unfold_lanes(folded):
    return jnp.concatenate([folded[8 * b : 8 * (b + 1)] for b in range(4)], axis=1)


def group_sum(rows):
    folded = fold_lanes(rows)
    for step in (1, 2, 4, 8):
        folded = butterfly(folded, step)
    return folded


def pack_groups(folded):
    lanes = lane_iota((8, HALF))
    packed = jnp.zeros((8, HALF), F32)
    for b in range(4):
        packed = jnp.where((lanes & 3) == b, folded[8 * b : 8 * (b + 1)], packed)
    return packed


def unpack_groups(packed):
    lanes = lane_iota((8, HALF))
    blocks = []
    for b in range(4):
        block = jnp.where((lanes & 3) == b, packed, 0.0)
        block = butterfly(butterfly(block, 1), 2)
        blocks.append(block)
    return jnp.concatenate(blocks, axis=1)


def rows_of(parts):
    zeros = jnp.zeros((8 - len(parts), parts[0].shape[1]), F32)
    return jnp.concatenate(parts + [zeros], axis=0)


def tile_stats(ref):
    sums = rows_of(
        [jnp.sum(ref[TILE * j : TILE * (j + 1), :], axis=0, keepdims=True) for j in range(3)]
    )
    total = group_sum(sums)
    means = unfold_lanes(total * (1.0 / (TILE * GROUP)))
    seconds = []
    for j in range(3):
        off = ref[TILE * j : TILE * (j + 1), :] - means[j : j + 1]
        seconds.append(jnp.sum(off * off, axis=0, keepdims=True))
    spread = group_sum(rows_of(seconds))
    return pack_groups(total) + pltpu.roll(pack_groups(spread), 4, 0)


def image_stats(win, stat, me, starts, ends):
    rows = win.shape[0] + 8
    table = jnp.concatenate([win[...], stat[...]], axis=0)
    row = lax.broadcasted_iota(jnp.int32, (rows, HALF), 0)
    slot = row >> 3
    tile_row = row & 7
    offset = jnp.where(slot >= WINDOW, slot - WINDOW + 1, slot - WINDOW)
    offset = jnp.where(slot >= PEERS, 0, offset)
    tile = 3 * (me + offset) + tile_row
    second = pltpu.roll(table.reshape(rows // 8, 8, HALF), 4, 1).reshape(rows, HALF)
    tile_mean = table * (1.0 / (TILE * GROUP))
    means, inverses = [], []
    for j in range(3):
        member = (tile >= starts[j]) & (tile < ends[j]) & (tile_row < 3)
        count = jnp.full((1, HALF), (ends[j] - starts[j]) * (TILE * GROUP), jnp.int32).astype(F32)
        mean = jnp.sum(jnp.where(member, table, 0.0), axis=0, keepdims=True) / count
        away = tile_mean - mean
        moment = second + (TILE * GROUP) * (away * away)
        spread = jnp.sum(jnp.where(member, moment, 0.0), axis=0, keepdims=True) / count
        means.append(mean)
        inverses.append(lax.rsqrt(spread + EPS))
    packed = rows_of(means) + pltpu.roll(rows_of(inverses), 4, 0)
    return unpack_groups(packed)


def kernel(
    counts,
    widths,
    latents,
    weight,
    bias,
    gain,
    shift,
    hidden,
    coef_out,
    local,
    halo,
    taps_a,
    taps_b,
    taps_y,
    acts,
    total,
    w_high,
    w_low,
    coef,
    stat1,
    stat2,
    win1,
    win2,
    local_sem,
    halo_send,
    halo_recv,
    stat_send,
    stat_recv,
    send_sem,
    recv_sem,
):
    t = lax.axis_index("tiles")
    s = lax.axis_index("sub")
    me = t * 8 + s
    z, x = t // 4, t % 4
    y, core = s // 2, s % 2

    def at(index):
        p = lax.rem(index + 256, 256)
        return (p // 8, p % 8)

    right = {
        "z+": (lax.rem(z + 1, 8) * 4 + x, s),
        "z-": (lax.rem(z + 7, 8) * 4 + x, s),
        "x+": (z * 4 + lax.rem(x + 1, 4), s),
        "x-": (z * 4 + lax.rem(x + 3, 4), s),
        "x2": (z * 4 + lax.rem(x + 2, 4), s),
        "y+": (t, lax.rem(y + 1, 4) * 2 + core),
        "y-": (t, lax.rem(y + 3, 4) * 2 + core),
        "c": (t, s + 1 - 2 * core),
    }

    def z_row(dz):
        return lax.rem(z + dz + 8, 8) * 4

    def row_of(dz, dx):
        return z_row(dz) + lax.rem(x + dx + 4, 4)

    odd = z % 2

    def s_row(ds):
        return z_row((1 - 2 * odd) * ds)

    barrier = pltpu.get_barrier_semaphore()

    def greet(step, carry):
        for sign in (1, -1):
            pl.semaphore_signal(barrier, inc=1, device_id=at(me + sign * step), device_id_type=MESH)
        return carry

    for name in ("z+", "z-", "x+", "x-", "x2", "y+", "y-"):
        pl.semaphore_signal(barrier, inc=1, device_id=right[name], device_id_type=MESH)
    lax.fori_loop(1, WINDOW + 1, greet, 0)

    load = pltpu.make_async_copy(latents, local, local_sem.at[0])
    load.start()

    own_a = pltpu.make_async_copy(weight.at[pl.ds(0, 1)], taps_a.at[t], local_sem.at[1])
    own_b = pltpu.make_async_copy(weight.at[pl.ds(1, 4)], taps_b.at[t], local_sem.at[1])
    own_y = pltpu.make_async_copy(weight.at[5 + y], taps_y.at[y, t], local_sem.at[2])

    @pl.when(core == 0)
    def _():
        own_y.start()
        own_a.start()

    @pl.when(core == 1)
    def _():
        own_b.start()

    tiles = [3 * me + j for j in range(3)]
    starts = [me * 0] * 3
    ends = [me * 0] * 3
    width = [me * 0 + 32] * 3
    begin = me * 0

    def place(i, carry):
        begin, starts, ends, width = carry
        end = begin + counts[i]
        inside = [(tile >= begin) & (tile < end) for tile in tiles]
        starts = [jnp.where(hit, begin, old) for hit, old in zip(inside, starts)]
        ends = [jnp.where(hit, end, old) for hit, old in zip(inside, ends)]
        width = [jnp.where(hit, widths[i], old) for hit, old in zip(inside, width)]
        return end, starts, ends, width

    _, starts, ends, width = lax.fori_loop(
        0, counts.shape[0], place, (begin, starts, ends, width)
    )

    def piece(part):
        kind, taps, first, count = part
        if kind == "y":
            return taps_y.at[pl.ds(taps[0], taps[1]), pl.ds(first, count)]
        ref = taps_a if kind == "a" else taps_b
        return ref.at[pl.ds(first, count), pl.ds(taps[0], taps[1])]

    sent = {0: [], 1: []}

    def remote(part, way, send_index, recv_index):
        ref = piece(part)
        return pltpu.make_async_remote_copy(
            src_ref=ref,
            dst_ref=ref,
            send_sem=send_sem.at[send_index],
            recv_sem=recv_sem.at[recv_index],
            device_id=right[way],
            device_id_type=MESH,
        )

    def send(owner, part, way, recv):
        remote(part, way, len(sent[owner]), recv).start()
        sent[owner].append((part[0], part[1][1], part[3]))

    def arrived(part, recv):
        remote(part, "c", 0, recv).wait_recv()

    group_of = {0: 0, -1: 1, 1: 2, -2: 3, 2: 4, -3: 5, 3: 6, 4: 7}
    a_all, b_all = (0, 1), (0, 4)
    onward = ("z+", "z-")

    def a_part(kind, first, count):
        return (kind, (y, 1) if kind == "y" else a_all, first, count)

    def a_start():
        own_y.wait()
        own_a.wait()
        for k, kind in enumerate("ya"):
            send(0, a_part(kind, row_of(0, 0), 1), "x+", 3 * k)
            send(0, a_part(kind, row_of(0, 0), 1), "x-", 3 * k + 1)
            send(0, a_part(kind, row_of(0, 0), 1), "x2", 3 * k + 2)

    def a_near(kind):
        k = "ya".index(kind)
        for way in range(2):
            arrived(a_part(kind, row_of(0, 1 if way else -1), 1), 3 * k + way)

    def a_far(kind):
        k = "ya".index(kind)
        arrived(a_part(kind, row_of(0, 2), 1), 3 * k + 2)
        for h in range(2):
            for way in range(2):
                part = a_part(kind, z_row(0) + 2 * h, 2)
                send(0, part, onward[way], 6 + 14 * k + 6 * way + h)
        a_done(kind, 0)

    def a_done(kind, dz):
        g = group_of[dz]
        part = a_part(kind, s_row(dz), 4)
        if kind == "y":
            send(0, part, "y+", 34 + 4 * g)
            send(0, part, "y-", 34 + 4 * g + 1)
        else:
            send(0, part, "c", 56 + g)

    def a_z(kind, d, way, h):
        k = "ya".index(kind)
        base = 6 + 14 * k
        if d == 4:
            arrived(a_part(kind, z_row(4) + 2 * h, 2), base + 12 + h)
            return
        part = a_part(kind, z_row(d if way else -d) + 2 * h, 2)
        arrived(part, base + 6 * way + 2 * (d - 1) + h)
        if d < 3:
            send(0, part, onward[way], base + 6 * way + 2 * d + h)
        elif way == h:
            send(0, part, onward[way], base + 12 + h)

    def y_near(dz, way):
        g = group_of[dz]
        tap = lax.rem(y + (1 if way else 3), 4)
        arrived(("y", (tap, 1), s_row(dz), 4), 34 + 4 * g + way)
        send(0, ("y", (tap, 1), s_row(dz) + 2 * way, 2), "y-" if way else "y+", 34 + 4 * g + 2 + way)

    def y_far(dz):
        g = group_of[dz]
        tap = lax.rem(y + 2, 4)
        for way in range(2):
            arrived(("y", (tap, 1), s_row(dz) + 2 * way, 2), 34 + 4 * g + 2 + way)
        send(0, ("y", (0, 4), s_row(dz), 4), "c", 64 + g)

    def b_halves(g):
        return ((0, 2), (2, 2))

    def b_spread(dz):
        g = group_of[dz]
        if 0 < abs(dz) < 4:
            g = 2 * dz - odd if dz > 0 else -2 * dz - 1 + odd
        part = ("b", b_all, row_of(dz, 0), 1)
        send(1, part, "x+", 8 + 4 * g)
        send(1, part, "x-", 8 + 4 * g + 1)

    def b_start():
        own_b.wait()
        part = ("b", b_all, row_of(0, 0), 1)
        send(1, part, "z+", 0)
        send(1, part, "z-", 3)
        b_spread(0)

    def b_z(d, way):
        dz = d if way else -d
        part = ("b", b_all, row_of(dz, 0), 1)
        arrived(part, 3 * way + d - 1)
        if d < 3:
            send(1, part, onward[way], 3 * way + d)
        else:
            send(1, ("b", b_halves(0)[way], row_of(dz, 0), 1), onward[way], 6 + way)
        b_spread(dz)

    def b_last():
        for way in range(2):
            arrived(("b", b_halves(0)[way], row_of(4, 0), 1), 6 + way)
        b_spread(4)

    def b_near(dz):
        g = group_of[dz]
        for way in range(2):
            first = s_row(dz) + lax.rem(x + (1 if way else 3), 4)
            arrived(("b", b_all, first, 1), 8 + 4 * g + way)
            send(1, ("b", b_halves(g)[way], first, 1), "x-" if way else "x+", 8 + 4 * g + 2 + way)

    def b_far(dz):
        g = group_of[dz]
        for way in range(2):
            arrived(("b", b_halves(g)[way], s_row(dz) + lax.rem(x + 2, 4), 1), 8 + 4 * g + 2 + way)
        send(1, ("b", b_all, s_row(dz), 4), "c", 66 + g)

    steps = {
        step.__name__: step
        for step in (
            a_start, a_near, a_far, a_done, a_z, y_near, y_far, b_start, b_z, b_last, b_near, b_far
        )
    }

    def serve(lists):
        for owner in range(2):
            if lists[owner]:

                @pl.when(core == owner)
                def _(owner=owner):
                    for name, *values in lists[owner]:
                        steps[name](*values)

    def serve_at(slot):
        if slot in SERVE:
            serve(SERVE[slot])

    def pair_arrived(groups, shared):
        @pl.when(core == 0)
        def _():
            for dz in groups if shared else ():
                arrived(("b", b_all, s_row(dz), 4), 66 + group_of[dz])

        @pl.when(core == 1)
        def _():
            for dz in groups:
                if shared:
                    arrived(("a", a_all, s_row(dz), 4), 56 + group_of[dz])
                else:
                    arrived(("y", (0, 4), s_row(dz), 4), 64 + group_of[dz])

    load.wait()
    stat1[...] = tile_stats(local)
    for h in range(8):
        rows = pl.ds(96 * h, 96)
        total[rows, :] = jnp.broadcast_to(bias[...], (96, 512))

    pl.semaphore_wait(barrier, PEERS + 7)
    serve(START)
    up = pltpu.make_async_remote_copy(
        src_ref=latents.at[pl.ds(5 * HALF, HALF), :],
        dst_ref=halo.at[0],
        send_sem=halo_send.at[0],
        recv_sem=halo_recv.at[0],
        device_id=at(me + 1),
        device_id_type=MESH,
    )
    down = pltpu.make_async_remote_copy(
        src_ref=latents.at[pl.ds(0, HALF), :],
        dst_ref=halo.at[1],
        send_sem=halo_send.at[1],
        recv_sem=halo_recv.at[1],
        device_id=at(me - 1),
        device_id_type=MESH,
    )

    def share(stat, win, which):
        def one(step, carry):
            for slot, to in ((WINDOW - step, me + step), (WINDOW - 1 + step, me - step)):
                pltpu.make_async_remote_copy(
                    src_ref=stat,
                    dst_ref=win.at[pl.ds(pl.multiple_of(slot * 8, 8), 8), :],
                    send_sem=stat_send.at[which],
                    recv_sem=stat_recv.at[which],
                    device_id=at(to),
                    device_id_type=MESH,
                ).start()
            return carry

        lax.fori_loop(1, WINDOW + 1, one, 0)

    def collect(win, which):
        ref = win
        both = pltpu.make_async_remote_copy(
            src_ref=ref,
            dst_ref=ref,
            send_sem=stat_send.at[which],
            recv_sem=stat_recv.at[which],
            device_id=at(me + 1),
            device_id_type=MESH,
        )
        both.wait_send()
        both.wait_recv()

    share(stat1, win1, 0)
    up.start()
    down.start()
    serve_at("stats")
    collect(win1, 0)
    coef[...] = image_stats(win1, stat1, me, starts, ends)
    up.wait()
    down.wait()

    def act_block(source, j, wide, stores):
        row = lax.broadcasted_iota(jnp.int32, (HALF, HALF), 0)
        column = row & (wide - 1)
        has_left = column != 0
        has_right = column != wide - 1
        for b in range(4):
            lanes = pl.ds(HALF * b, HALF)
            mean = coef[pl.ds(j, 1), lanes]
            scale = coef[pl.ds(j + 4, 1), lanes] * gain[:, HALF * b : HALF * (b + 1)]
            value = (source(lanes) - mean) * scale + shift[:, HALF * b : HALF * (b + 1)]
            act = value / (1.0 + jnp.exp(-value))
            shifted = (
                jnp.where(has_left, pltpu.roll(act, 1, 0), 0.0),
                act,
                jnp.where(has_right, pltpu.roll(act, HALF - 1, 0), 0.0),
            )
            for dx in range(3):
                high = shifted[dx].astype(BF16)
                low = (shifted[dx] - high.astype(F32)).astype(BF16)
                for base, valid in stores:
                    rows = pl.ds(base, HALF)
                    if valid is None:
                        acts[dx, 0, rows, lanes] = high
                        acts[dx, 1, rows, lanes] = low
                    else:
                        keep = jnp.where(valid, 1.0, 0.0).astype(F32)
                        acts[dx, 0, rows, lanes] = (high.astype(F32) * keep).astype(BF16)
                        acts[dx, 1, rows, lanes] = (low.astype(F32) * keep).astype(BF16)

    act_block(lambda lanes: halo[0, :, lanes], 0, width[0], [(0, tiles[0] > starts[0])])
    serve_at("act0")
    act_block(lambda lanes: halo[1, :, lanes], 2, width[2], [(2 * 512 + 384, tiles[2] + 1 < ends[2])])
    serve_at("act1")
    for q in range(6):
        j, half = q // 2, q % 2
        stores = [(j * 512 + HALF + half * HALF, None)]
        if half == 0 and j > 0:
            stores.append(((j - 1) * 512 + 384, tiles[j] > starts[j]))
        if half == 1 and j < 2:
            stores.append(((j + 1) * 512, tiles[j + 1] > starts[j + 1]))
        act_block(lambda lanes, q=q: local[HALF * q : HALF * (q + 1), lanes], j, width[j], stores)
        serve_at(f"act{q + 2}")

    first = z // 2
    order = [
        first,
        lax.rem(first + 3 + 2 * odd, 4),
        lax.rem(first + 1 + 2 * odd, 4),
        lax.rem(first + 2, 4),
    ]
    groups = [(0, 1), (-1, -2), (2, 3), (-3, 4)]

    def split_weights(chunk, taps):
        def fixed(c):
            for tap in taps:
                if tap < 1:
                    value = taps_a[8 * c : 8 * c + 8, tap : tap + 1]
                elif tap < 5:
                    value = taps_b[8 * c : 8 * c + 8, tap - 1 : tap]
                else:
                    value = taps_y[tap - 5 : tap - 4, 8 * c : 8 * c + 8]
                value = value.reshape(HALF, 512)
                to = pl.ds(tap * HALF, HALF)
                high = value.astype(BF16)
                w_high[to, :] = high
                w_low[to, :] = (value - high.astype(F32)).astype(BF16)

        for c in range(4):
            pl.when(chunk == c)(functools.partial(fixed, c))

    def multiply(chunk, taps, j):
        lanes = pl.ds(pl.multiple_of(chunk * HALF, HALF), HALF)
        wide = width[j]
        is_wide, is_middle = wide == 128, wide == 64

        def columns(part):
            blocks = []
            for tap in taps:
                dy, dx = tap // 3 - 1, tap % 3
                base = j * 512 + HALF
                if dy == 0:
                    blocks.append(acts[dx, part, pl.ds(base, TILE), lanes])
                    continue
                near = acts[dx, part, pl.ds(base + 32 * dy, TILE), lanes]
                middle = acts[dx, part, pl.ds(base + 64 * dy, TILE), lanes]
                far = acts[dx, part, pl.ds(base + 128 * dy, TILE), lanes]
                blocks.append(jnp.where(is_wide, far, jnp.where(is_middle, middle, near)))
            return jnp.concatenate(blocks, axis=1)

        weight_rows = pl.ds(taps[0] * HALF, len(taps) * HALF)
        high = columns(0)
        low = columns(1)
        out = jnp.dot(high, w_high[weight_rows, :], preferred_element_type=F32)
        out += jnp.dot(low, w_high[weight_rows, :], preferred_element_type=F32)
        out += jnp.dot(high, w_low[weight_rows, :], preferred_element_type=F32)
        rows = pl.ds(pl.multiple_of(j * TILE, TILE), TILE)
        total[rows, :] += out

    for k in range(4):
        for part, taps in enumerate((range(0, 5), range(5, 9))):
            serve_at(f"pre{k}{part}")
            pair_arrived(groups[k], part == 0)
            split_weights(order[k], taps)
            for j in range(3):
                multiply(order[k], taps, j)
                serve_at(f"post{k}{part}{j}")

    store = pltpu.make_async_copy(total, hidden, local_sem.at[6])
    store.start()
    stat2[...] = tile_stats(total)
    share(stat2, win2, 1)
    for owner in range(2):

        @pl.when(core == owner)
        def _(owner=owner):
            for index, (kind, taps, count) in enumerate(sent[owner]):
                remote((kind, (0, taps), 0, count), "c", index, 0).wait_send()

    collect(win2, 1)
    coef_out[...] = image_stats(win2, stat2, me, starts, ends)
    store.wait()


def shards(latents, weight, bias, gain1, shift1, gain2, shift2, tile_counts, widths):
    vmem = pl.BlockSpec(memory_space=pltpu.VMEM)
    smem = pl.BlockSpec(memory_space=pltpu.SMEM)
    hbm = pl.BlockSpec(memory_space=pl.ANY)
    dma = pltpu.SemaphoreType.DMA
    pixels, channels = latents.shape
    hidden, coef = pl.pallas_call(
        kernel,
        out_shape=(
            jax.ShapeDtypeStruct((pixels, channels), F32),
            jax.ShapeDtypeStruct((8, channels), F32),
        ),
        in_specs=[smem, smem, hbm, hbm, vmem, vmem, vmem],
        out_specs=(hbm, vmem),
        scratch_shapes=[
            pltpu.VMEM((pixels, channels), F32),
            pltpu.VMEM((2, HALF, channels), F32),
            pltpu.VMEM((32, 1, 16, channels), F32),
            pltpu.VMEM((32, 4, 16, channels), F32),
            pltpu.VMEM((4, 32, 16, channels), F32),
            pltpu.VMEM((3, 2, 1536, channels), BF16),
            pltpu.VMEM((pixels, channels), F32),
            pltpu.VMEM((9 * HALF, channels), BF16),
            pltpu.VMEM((9 * HALF, channels), BF16),
            pltpu.VMEM((8, channels), F32),
            pltpu.VMEM((8, HALF), F32),
            pltpu.VMEM((8, HALF), F32),
            pltpu.VMEM((8 * PEERS, HALF), F32),
            pltpu.VMEM((8 * PEERS, HALF), F32),
            dma((7,)),
            dma((2,)),
            dma((2,)),
            dma((2,)),
            dma((2,)),
            dma((96,)),
            dma((80,)),
        ],
        compiler_params=pltpu.CompilerParams(
            collective_id=0, has_side_effects=True, vmem_limit_bytes=60 << 20
        ),
        name="block",
    )(
        tile_counts,
        widths,
        latents,
        jnp.transpose(weight, (1, 0, 2)),
        bias.reshape(1, -1),
        gain1.reshape(1, -1),
        shift1.reshape(1, -1),
    )
    centred = hidden.reshape(3, TILE, channels) - coef[0:3, None, :]
    value = centred * (coef[4:7, None, :] * gain2) + shift2
    return jax.nn.silu(value).reshape(pixels, channels)


def solution(mesh):
    return jax.shard_map(
        shards,
        mesh=mesh,
        in_specs=(
            P(("tiles", "sub"), None),
            P("tiles", None, None),
            P(),
            P(),
            P(),
            P(),
            P(),
            P(),
            P(),
        ),
        out_specs=P(("tiles", "sub"), None),
        check_vma=False,
    )
```

```python
import functools

import jax
import jax.numpy as jnp
from jax import lax
from jax.experimental import pallas as pl
from jax.experimental.pallas import tpu as pltpu
from jax.sharding import PartitionSpec as P

MESH = pl.DeviceIdType.MESH
F32 = jnp.float32
BF16 = jnp.bfloat16

TILE = 256
GROUP = 16
HALF = 128
EPS = 1e-06
WINDOW = 21
PEERS = 2 * WINDOW


START = ([("a_start",)], [("b_start",)])
SERVE = {
    "stats": (
        [("a_near", "y"), ("a_near", "a"), ("a_far", "y")],
        [("b_z", 1, 0), ("b_z", 1, 1)],
    ),
    "act0": (
        [("a_far", "a")],
        [("b_near", 0)],
    ),
    "act6": (
        [("y_near", 0, 0), ("y_near", 0, 1)],
        [("b_z", 2, 0), ("b_z", 2, 1)],
    ),
    "act7": (
        [("a_z", "y", 1, 0, 0), ("a_z", "y", 1, 1, 0)],
        [],
    ),
    "pre00": (
        [("a_z", "y", 1, 0, 1), ("a_z", "y", 1, 1, 1), ("a_done", "y", 1), ("a_done", "y", -1), ("a_z", "a", 1, 0, 0), ("a_z", "a", 1, 1, 0), ("a_z", "a", 1, 0, 1), ("a_z", "a", 1, 1, 1), ("a_done", "a", 1), ("a_done", "a", -1), ("y_far", 0), ("a_z", "y", 2, 0, 0), ("a_z", "y", 2, 1, 0), ("y_near", 1, 0), ("y_near", 1, 1), ("a_z", "y", 2, 0, 1), ("a_z", "y", 2, 1, 1), ("a_done", "y", -2), ("a_done", "y", 2), ("a_z", "a", 2, 0, 0), ("a_z", "a", 2, 1, 0), ("y_near", -1, 0), ("y_near", -1, 1), ("a_z", "a", 2, 0, 1), ("a_z", "a", 2, 1, 1), ("a_done", "a", -2), ("a_done", "a", 2), ("y_far", 1), ("a_z", "y", 3, 0, 0), ("a_z", "y", 3, 1, 0)],
        [("b_near", -1), ("b_near", 1), ("b_far", 0), ("b_z", 3, 0), ("b_z", 3, 1), ("b_near", -2), ("b_near", 2), ("b_far", -1), ("b_far", 1), ("b_last",)],
    ),
    "post000": (
        [("a_z", "y", 3, 0, 1), ("a_z", "y", 3, 1, 1), ("a_done", "y", 3), ("a_done", "y", -3), ("y_near", -2, 0), ("y_near", -2, 1)],
        [],
    ),
    "post001": (
        [("a_z", "a", 3, 0, 0), ("a_z", "a", 3, 1, 0)],
        [("b_near", 3), ("b_near", -3)],
    ),
    "post002": (
        [("a_z", "a", 3, 0, 1), ("a_z", "a", 3, 1, 1), ("a_done", "a", 3), ("a_done", "a", -3), ("y_near", 2, 0), ("y_near", 2, 1)],
        [("b_far", -2), ("b_far", 2)],
    ),
    "post010": (
        [("a_z", "y", 4, 0, 0), ("y_far", -1)],
        [],
    ),
    "post011": (
        [("a_z", "y", 4, 0, 1), ("a_done", "y", 4)],
        [("b_near", 4)],
    ),
    "post012": (
        [("a_z", "a", 4, 0, 0), ("y_near", 3, 0), ("y_near", 3, 1)],
        [],
    ),
    "post100": (
        [("a_z", "a", 4, 0, 1), ("a_done", "a", 4)],
        [("b_far", 3), ("b_far", -3)],
    ),
    "post101": (
        [("y_near", -3, 0), ("y_near", -3, 1)],
        [],
    ),
    "post102": (
        [("y_far", -2)],
        [("b_far", 4)],
    ),
    "pre11": (
        [("y_far", 2)],
        [],
    ),
    "post110": (
        [("y_near", 4, 0), ("y_near", 4, 1)],
        [],
    ),
    "post111": (
        [("y_far", 3)],
        [],
    ),
    "post112": (
        [("y_far", -3)],
        [],
    ),
    "post201": (
        [("y_far", 4)],
        [],
    ),
}


def lane_iota(shape):
    return lax.broadcasted_iota(jnp.int32, shape, len(shape) - 1)


def butterfly(values, step):
    lanes = lane_iota(values.shape)
    up = pltpu.roll(values, step, 1)
    down = pltpu.roll(values, HALF - step, 1)
    return values + jnp.where((lanes & step) != 0, up, down)


def fold_lanes(rows):
    return jnp.concatenate([rows[:, HALF * b : HALF * (b + 1)] for b in range(4)], axis=0)


def unfold_lanes(folded):
    return jnp.concatenate([folded[8 * b : 8 * (b + 1)] for b in range(4)], axis=1)


def group_sum(rows):
    folded = fold_lanes(rows)
    for step in (1, 2, 4, 8):
        folded = butterfly(folded, step)
    return folded


def pack_groups(folded):
    lanes = lane_iota((8, HALF))
    packed = jnp.zeros((8, HALF), F32)
    for b in range(4):
        packed = jnp.where((lanes & 3) == b, folded[8 * b : 8 * (b + 1)], packed)
    return packed


def unpack_groups(packed):
    lanes = lane_iota((8, HALF))
    blocks = []
    for b in range(4):
        block = jnp.where((lanes & 3) == b, packed, 0.0)
        block = butterfly(butterfly(block, 1), 2)
        blocks.append(block)
    return jnp.concatenate(blocks, axis=1)


def rows_of(parts):
    zeros = jnp.zeros((8 - len(parts), parts[0].shape[1]), F32)
    return jnp.concatenate(parts + [zeros], axis=0)


def tile_stats(ref):
    sums = rows_of(
        [jnp.sum(ref[TILE * j : TILE * (j + 1), :], axis=0, keepdims=True) for j in range(3)]
    )
    total = group_sum(sums)
    means = unfold_lanes(total * (1.0 / (TILE * GROUP)))
    seconds = []
    for j in range(3):
        off = ref[TILE * j : TILE * (j + 1), :] - means[j : j + 1]
        seconds.append(jnp.sum(off * off, axis=0, keepdims=True))
    spread = group_sum(rows_of(seconds))
    return pack_groups(total) + pltpu.roll(pack_groups(spread), 4, 0)


def image_stats(win, stat, me, starts, ends):
    rows = win.shape[0] + 8
    table = jnp.concatenate([win[...], stat[...]], axis=0)
    row = lax.broadcasted_iota(jnp.int32, (rows, HALF), 0)
    slot = row >> 3
    tile_row = row & 7
    offset = jnp.where(slot >= WINDOW, slot - WINDOW + 1, slot - WINDOW)
    offset = jnp.where(slot >= PEERS, 0, offset)
    tile = 3 * (me + offset) + tile_row
    second = pltpu.roll(table.reshape(rows // 8, 8, HALF), 4, 1).reshape(rows, HALF)
    tile_mean = table * (1.0 / (TILE * GROUP))
    means, inverses = [], []
    for j in range(3):
        member = (tile >= starts[j]) & (tile < ends[j]) & (tile_row < 3)
        count = jnp.full((1, HALF), (ends[j] - starts[j]) * (TILE * GROUP), jnp.int32).astype(F32)
        mean = jnp.sum(jnp.where(member, table, 0.0), axis=0, keepdims=True) / count
        away = tile_mean - mean
        moment = second + (TILE * GROUP) * (away * away)
        spread = jnp.sum(jnp.where(member, moment, 0.0), axis=0, keepdims=True) / count
        means.append(mean)
        inverses.append(lax.rsqrt(spread + EPS))
    packed = rows_of(means) + pltpu.roll(rows_of(inverses), 4, 0)
    return unpack_groups(packed)


def kernel(
    counts,
    widths,
    latents,
    weight,
    bias,
    gain,
    shift,
    gain2,
    hidden,
    mean_out,
    scale_out,
    local,
    halo,
    taps_a,
    taps_b,
    taps_y,
    acts,
    total,
    w_high,
    w_low,
    coef,
    stat1,
    stat2,
    win1,
    win2,
    local_sem,
    halo_send,
    halo_recv,
    stat_send,
    stat_recv,
    send_sem,
    recv_sem,
):
    t = lax.axis_index("tiles")
    s = lax.axis_index("sub")
    me = t * 8 + s
    z, x = t // 4, t % 4
    y, core = s // 2, s % 2

    def at(index):
        p = lax.rem(index + 256, 256)
        return (p // 8, p % 8)

    right = {
        "z+": (lax.rem(z + 1, 8) * 4 + x, s),
        "z-": (lax.rem(z + 7, 8) * 4 + x, s),
        "x+": (z * 4 + lax.rem(x + 1, 4), s),
        "x-": (z * 4 + lax.rem(x + 3, 4), s),
        "x2": (z * 4 + lax.rem(x + 2, 4), s),
        "y+": (t, lax.rem(y + 1, 4) * 2 + core),
        "y-": (t, lax.rem(y + 3, 4) * 2 + core),
        "c": (t, s + 1 - 2 * core),
    }

    def z_row(dz):
        return lax.rem(z + dz + 8, 8) * 4

    def row_of(dz, dx):
        return z_row(dz) + lax.rem(x + dx + 4, 4)

    odd = z % 2

    def s_row(ds):
        return z_row((1 - 2 * odd) * ds)

    barrier = pltpu.get_barrier_semaphore()

    def greet(step, carry):
        for sign in (1, -1):
            pl.semaphore_signal(barrier, inc=1, device_id=at(me + sign * step), device_id_type=MESH)
        return carry

    for name in ("z+", "z-", "x+", "x-", "x2", "y+", "y-"):
        pl.semaphore_signal(barrier, inc=1, device_id=right[name], device_id_type=MESH)
    lax.fori_loop(1, WINDOW + 1, greet, 0)

    load = pltpu.make_async_copy(latents, local, local_sem.at[0])
    load.start()

    own_a = pltpu.make_async_copy(weight.at[pl.ds(0, 1)], taps_a.at[t], local_sem.at[1])
    own_b = pltpu.make_async_copy(weight.at[pl.ds(1, 4)], taps_b.at[t], local_sem.at[1])
    own_y = pltpu.make_async_copy(weight.at[5 + y], taps_y.at[y, t], local_sem.at[2])

    @pl.when(core == 0)
    def _():
        own_y.start()
        own_a.start()

    @pl.when(core == 1)
    def _():
        own_b.start()

    tiles = [3 * me + j for j in range(3)]
    starts = [me * 0] * 3
    ends = [me * 0] * 3
    width = [me * 0 + 32] * 3
    begin = me * 0

    def place(i, carry):
        begin, starts, ends, width = carry
        end = begin + counts[i]
        inside = [(tile >= begin) & (tile < end) for tile in tiles]
        starts = [jnp.where(hit, begin, old) for hit, old in zip(inside, starts)]
        ends = [jnp.where(hit, end, old) for hit, old in zip(inside, ends)]
        width = [jnp.where(hit, widths[i], old) for hit, old in zip(inside, width)]
        return end, starts, ends, width

    _, starts, ends, width = lax.fori_loop(
        0, counts.shape[0], place, (begin, starts, ends, width)
    )

    def piece(part):
        kind, taps, first, count = part
        if kind == "y":
            return taps_y.at[pl.ds(taps[0], taps[1]), pl.ds(first, count)]
        ref = taps_a if kind == "a" else taps_b
        return ref.at[pl.ds(first, count), pl.ds(taps[0], taps[1])]

    sent = {0: [], 1: []}

    def remote(part, way, send_index, recv_index):
        ref = piece(part)
        return pltpu.make_async_remote_copy(
            src_ref=ref,
            dst_ref=ref,
            send_sem=send_sem.at[send_index],
            recv_sem=recv_sem.at[recv_index],
            device_id=right[way],
            device_id_type=MESH,
        )

    def send(owner, part, way, recv):
        remote(part, way, len(sent[owner]), recv).start()
        sent[owner].append((part[0], part[1][1], part[3]))

    def arrived(part, recv):
        remote(part, "c", 0, recv).wait_recv()

    group_of = {0: 0, -1: 1, 1: 2, -2: 3, 2: 4, -3: 5, 3: 6, 4: 7}
    a_all, b_all = (0, 1), (0, 4)
    onward = ("z+", "z-")

    def a_part(kind, first, count):
        return (kind, (y, 1) if kind == "y" else a_all, first, count)

    def a_start():
        own_y.wait()
        own_a.wait()
        for k, kind in enumerate("ya"):
            send(0, a_part(kind, row_of(0, 0), 1), "x+", 3 * k)
            send(0, a_part(kind, row_of(0, 0), 1), "x-", 3 * k + 1)
            send(0, a_part(kind, row_of(0, 0), 1), "x2", 3 * k + 2)

    def a_near(kind):
        k = "ya".index(kind)
        for way in range(2):
            arrived(a_part(kind, row_of(0, 1 if way else -1), 1), 3 * k + way)

    def a_far(kind):
        k = "ya".index(kind)
        arrived(a_part(kind, row_of(0, 2), 1), 3 * k + 2)
        for h in range(2):
            for way in range(2):
                part = a_part(kind, z_row(0) + 2 * h, 2)
                send(0, part, onward[way], 6 + 14 * k + 6 * way + h)
        a_done(kind, 0)

    def a_done(kind, dz):
        g = group_of[dz]
        part = a_part(kind, s_row(dz), 4)
        if kind == "y":
            send(0, part, "y+", 34 + 4 * g)
            send(0, part, "y-", 34 + 4 * g + 1)
        else:
            send(0, part, "c", 56 + g)

    def a_z(kind, d, way, h):
        k = "ya".index(kind)
        base = 6 + 14 * k
        if d == 4:
            arrived(a_part(kind, z_row(4) + 2 * h, 2), base + 12 + h)
            return
        part = a_part(kind, z_row(d if way else -d) + 2 * h, 2)
        arrived(part, base + 6 * way + 2 * (d - 1) + h)
        if d < 3:
            send(0, part, onward[way], base + 6 * way + 2 * d + h)
        elif way == h:
            send(0, part, onward[way], base + 12 + h)

    def y_near(dz, way):
        g = group_of[dz]
        tap = lax.rem(y + (1 if way else 3), 4)
        arrived(("y", (tap, 1), s_row(dz), 4), 34 + 4 * g + way)
        send(0, ("y", (tap, 1), s_row(dz) + 2 * way, 2), "y-" if way else "y+", 34 + 4 * g + 2 + way)

    def y_far(dz):
        g = group_of[dz]
        tap = lax.rem(y + 2, 4)
        for way in range(2):
            arrived(("y", (tap, 1), s_row(dz) + 2 * way, 2), 34 + 4 * g + 2 + way)
        send(0, ("y", (0, 4), s_row(dz), 4), "c", 64 + g)

    def b_halves(g):
        return ((0, 2), (2, 2))

    def b_spread(dz):
        g = group_of[dz]
        if 0 < abs(dz) < 4:
            g = 2 * dz - odd if dz > 0 else -2 * dz - 1 + odd
        part = ("b", b_all, row_of(dz, 0), 1)
        send(1, part, "x+", 8 + 4 * g)
        send(1, part, "x-", 8 + 4 * g + 1)

    def b_start():
        own_b.wait()
        part = ("b", b_all, row_of(0, 0), 1)
        send(1, part, "z+", 0)
        send(1, part, "z-", 3)
        b_spread(0)

    def b_z(d, way):
        dz = d if way else -d
        part = ("b", b_all, row_of(dz, 0), 1)
        arrived(part, 3 * way + d - 1)
        if d < 3:
            send(1, part, onward[way], 3 * way + d)
        else:
            send(1, ("b", b_halves(0)[way], row_of(dz, 0), 1), onward[way], 6 + way)
        b_spread(dz)

    def b_last():
        for way in range(2):
            arrived(("b", b_halves(0)[way], row_of(4, 0), 1), 6 + way)
        b_spread(4)

    def b_near(dz):
        g = group_of[dz]
        for way in range(2):
            first = s_row(dz) + lax.rem(x + (1 if way else 3), 4)
            arrived(("b", b_all, first, 1), 8 + 4 * g + way)
            send(1, ("b", b_halves(g)[way], first, 1), "x-" if way else "x+", 8 + 4 * g + 2 + way)

    def b_far(dz):
        g = group_of[dz]
        for way in range(2):
            arrived(("b", b_halves(g)[way], s_row(dz) + lax.rem(x + 2, 4), 1), 8 + 4 * g + 2 + way)
        send(1, ("b", b_all, s_row(dz), 4), "c", 66 + g)

    steps = {
        step.__name__: step
        for step in (
            a_start, a_near, a_far, a_done, a_z, y_near, y_far, b_start, b_z, b_last, b_near, b_far
        )
    }

    def serve(lists):
        for owner in range(2):
            if lists[owner]:

                @pl.when(core == owner)
                def _(owner=owner):
                    for name, *values in lists[owner]:
                        steps[name](*values)

    def serve_at(slot):
        if slot in SERVE:
            serve(SERVE[slot])

    def pair_arrived(groups, shared):
        @pl.when(core == 0)
        def _():
            for dz in groups if shared else ():
                arrived(("b", b_all, s_row(dz), 4), 66 + group_of[dz])

        @pl.when(core == 1)
        def _():
            for dz in groups:
                if shared:
                    arrived(("a", a_all, s_row(dz), 4), 56 + group_of[dz])
                else:
                    arrived(("y", (0, 4), s_row(dz), 4), 64 + group_of[dz])

    load.wait()
    stat1[...] = tile_stats(local)
    for h in range(8):
        rows = pl.ds(96 * h, 96)
        total[rows, :] = jnp.broadcast_to(bias[...], (96, 512))

    pl.semaphore_wait(barrier, PEERS + 7)
    serve(START)
    up = pltpu.make_async_remote_copy(
        src_ref=latents.at[pl.ds(5 * HALF, HALF), :],
        dst_ref=halo.at[0],
        send_sem=halo_send.at[0],
        recv_sem=halo_recv.at[0],
        device_id=at(me + 1),
        device_id_type=MESH,
    )
    down = pltpu.make_async_remote_copy(
        src_ref=latents.at[pl.ds(0, HALF), :],
        dst_ref=halo.at[1],
        send_sem=halo_send.at[1],
        recv_sem=halo_recv.at[1],
        device_id=at(me - 1),
        device_id_type=MESH,
    )

    def share(stat, win, which):
        def one(step, carry):
            for slot, to in ((WINDOW - step, me + step), (WINDOW - 1 + step, me - step)):
                pltpu.make_async_remote_copy(
                    src_ref=stat,
                    dst_ref=win.at[pl.ds(pl.multiple_of(slot * 8, 8), 8), :],
                    send_sem=stat_send.at[which],
                    recv_sem=stat_recv.at[which],
                    device_id=at(to),
                    device_id_type=MESH,
                ).start()
            return carry

        lax.fori_loop(1, WINDOW + 1, one, 0)

    def collect(win, which):
        ref = win
        both = pltpu.make_async_remote_copy(
            src_ref=ref,
            dst_ref=ref,
            send_sem=stat_send.at[which],
            recv_sem=stat_recv.at[which],
            device_id=at(me + 1),
            device_id_type=MESH,
        )
        both.wait_send()
        both.wait_recv()

    share(stat1, win1, 0)
    up.start()
    down.start()
    serve_at("stats")
    collect(win1, 0)
    coef[...] = image_stats(win1, stat1, me, starts, ends)
    up.wait()
    down.wait()

    def act_block(source, j, wide, stores):
        row = lax.broadcasted_iota(jnp.int32, (HALF, HALF), 0)
        column = row & (wide - 1)
        has_left = column != 0
        has_right = column != wide - 1
        for b in range(4):
            lanes = pl.ds(HALF * b, HALF)
            mean = coef[pl.ds(j, 1), lanes]
            scale = coef[pl.ds(j + 4, 1), lanes] * gain[:, HALF * b : HALF * (b + 1)]
            value = (source(lanes) - mean) * scale + shift[:, HALF * b : HALF * (b + 1)]
            act = value / (1.0 + jnp.exp(-value))
            shifted = (
                jnp.where(has_left, pltpu.roll(act, 1, 0), 0.0),
                act,
                jnp.where(has_right, pltpu.roll(act, HALF - 1, 0), 0.0),
            )
            for dx in range(3):
                high = shifted[dx].astype(BF16)
                low = (shifted[dx] - high.astype(F32)).astype(BF16)
                for base, valid in stores:
                    rows = pl.ds(base, HALF)
                    if valid is None:
                        acts[dx, 0, rows, lanes] = high
                        acts[dx, 1, rows, lanes] = low
                    else:
                        keep = jnp.where(valid, 1.0, 0.0).astype(F32)
                        acts[dx, 0, rows, lanes] = (high.astype(F32) * keep).astype(BF16)
                        acts[dx, 1, rows, lanes] = (low.astype(F32) * keep).astype(BF16)

    act_block(lambda lanes: halo[0, :, lanes], 0, width[0], [(0, tiles[0] > starts[0])])
    serve_at("act0")
    act_block(lambda lanes: halo[1, :, lanes], 2, width[2], [(2 * 512 + 384, tiles[2] + 1 < ends[2])])
    serve_at("act1")
    for q in range(6):
        j, half = q // 2, q % 2
        stores = [(j * 512 + HALF + half * HALF, None)]
        if half == 0 and j > 0:
            stores.append(((j - 1) * 512 + 384, tiles[j] > starts[j]))
        if half == 1 and j < 2:
            stores.append(((j + 1) * 512, tiles[j + 1] > starts[j + 1]))
        act_block(lambda lanes, q=q: local[HALF * q : HALF * (q + 1), lanes], j, width[j], stores)
        serve_at(f"act{q + 2}")

    first = z // 2
    order = [
        first,
        lax.rem(first + 3 + 2 * odd, 4),
        lax.rem(first + 1 + 2 * odd, 4),
        lax.rem(first + 2, 4),
    ]
    groups = [(0, 1), (-1, -2), (2, 3), (-3, 4)]

    def split_weights(chunk, taps):
        def fixed(c):
            for tap in taps:
                if tap < 1:
                    value = taps_a[8 * c : 8 * c + 8, tap : tap + 1]
                elif tap < 5:
                    value = taps_b[8 * c : 8 * c + 8, tap - 1 : tap]
                else:
                    value = taps_y[tap - 5 : tap - 4, 8 * c : 8 * c + 8]
                value = value.reshape(HALF, 512)
                to = pl.ds(tap * HALF, HALF)
                high = value.astype(BF16)
                w_high[to, :] = high
                w_low[to, :] = (value - high.astype(F32)).astype(BF16)

        for c in range(4):
            pl.when(chunk == c)(functools.partial(fixed, c))

    def multiply(chunk, taps, j):
        lanes = pl.ds(pl.multiple_of(chunk * HALF, HALF), HALF)
        wide = width[j]
        is_wide, is_middle = wide == 128, wide == 64

        def columns(part):
            blocks = []
            for tap in taps:
                dy, dx = tap // 3 - 1, tap % 3
                base = j * 512 + HALF
                if dy == 0:
                    blocks.append(acts[dx, part, pl.ds(base, TILE), lanes])
                    continue
                near = acts[dx, part, pl.ds(base + 32 * dy, TILE), lanes]
                middle = acts[dx, part, pl.ds(base + 64 * dy, TILE), lanes]
                far = acts[dx, part, pl.ds(base + 128 * dy, TILE), lanes]
                blocks.append(jnp.where(is_wide, far, jnp.where(is_middle, middle, near)))
            return jnp.concatenate(blocks, axis=1)

        weight_rows = pl.ds(taps[0] * HALF, len(taps) * HALF)
        high = columns(0)
        low = columns(1)
        w1, w2 = w_high[weight_rows, :], w_low[weight_rows, :]
        out = jnp.dot(
            jnp.concatenate([high, low, high], axis=1),
            jnp.concatenate([w1, w1, w2], axis=0),
            preferred_element_type=F32,
        )
        rows = pl.ds(pl.multiple_of(j * TILE, TILE), TILE)
        total[rows, :] += out

    for k in range(4):
        for part, taps in enumerate((range(0, 5), range(5, 9))):
            serve_at(f"pre{k}{part}")
            pair_arrived(groups[k], part == 0)
            split_weights(order[k], taps)
            for j in range(3):
                multiply(order[k], taps, j)
                serve_at(f"post{k}{part}{j}")

    store = pltpu.make_async_copy(total, hidden, local_sem.at[6])
    store.start()
    stat2[...] = tile_stats(total)
    share(stat2, win2, 1)
    for owner in range(2):

        @pl.when(core == owner)
        def _(owner=owner):
            for index, (kind, taps, count) in enumerate(sent[owner]):
                remote((kind, (0, taps), 0, count), "c", index, 0).wait_send()

    collect(win2, 1)
    final = image_stats(win2, stat2, me, starts, ends)
    mean_out[...] = final[0:3]
    scale_out[...] = final[4:7] * gain2[...]
    store.wait()


def shards(latents, weight, bias, gain1, shift1, gain2, shift2, tile_counts, widths):
    vmem = pl.BlockSpec(memory_space=pltpu.VMEM)
    smem = pl.BlockSpec(memory_space=pltpu.SMEM)
    hbm = pl.BlockSpec(memory_space=pl.ANY)
    dma = pltpu.SemaphoreType.DMA
    pixels, channels = latents.shape
    hidden, mean, scale = pl.pallas_call(
        kernel,
        out_shape=(
            jax.ShapeDtypeStruct((pixels, channels), F32),
            jax.ShapeDtypeStruct((3, channels), F32),
            jax.ShapeDtypeStruct((3, channels), F32),
        ),
        in_specs=[smem, smem, hbm, hbm, vmem, vmem, vmem, vmem],
        out_specs=(hbm, vmem, vmem),
        scratch_shapes=[
            pltpu.VMEM((pixels, channels), F32),
            pltpu.VMEM((2, HALF, channels), F32),
            pltpu.VMEM((32, 1, 16, channels), F32),
            pltpu.VMEM((32, 4, 16, channels), F32),
            pltpu.VMEM((4, 32, 16, channels), F32),
            pltpu.VMEM((3, 2, 1536, channels), BF16),
            pltpu.VMEM((pixels, channels), F32),
            pltpu.VMEM((9 * HALF, channels), BF16),
            pltpu.VMEM((9 * HALF, channels), BF16),
            pltpu.VMEM((8, channels), F32),
            pltpu.VMEM((8, HALF), F32),
            pltpu.VMEM((8, HALF), F32),
            pltpu.VMEM((8 * PEERS, HALF), F32),
            pltpu.VMEM((8 * PEERS, HALF), F32),
            dma((7,)),
            dma((2,)),
            dma((2,)),
            dma((2,)),
            dma((2,)),
            dma((96,)),
            dma((80,)),
        ],
        compiler_params=pltpu.CompilerParams(
            collective_id=0, has_side_effects=True, vmem_limit_bytes=60 << 20
        ),
        name="block",
    )(
        tile_counts,
        widths,
        latents,
        jnp.transpose(weight, (1, 0, 2)),
        bias.reshape(1, -1),
        gain1.reshape(1, -1),
        shift1.reshape(1, -1),
        gain2.reshape(1, -1),
    )
    centred = hidden.reshape(3, TILE, channels) - mean[:, None, :]
    value = centred * scale[:, None, :] + shift2
    return jax.nn.silu(value).reshape(pixels, channels)


def solution(mesh):
    return jax.shard_map(
        shards,
        mesh=mesh,
        in_specs=(
            P(("tiles", "sub"), None),
            P("tiles", None, None),
            P(),
            P(),
            P(),
            P(),
            P(),
            P(),
            P(),
        ),
        out_specs=P(("tiles", "sub"), None),
        check_vma=False,
    )
```

```python
import functools

import jax
import jax.numpy as jnp
from jax import lax
from jax.experimental import pallas as pl
from jax.experimental.pallas import tpu as pltpu
from jax.sharding import PartitionSpec as P

MESH = pl.DeviceIdType.MESH
F32 = jnp.float32
BF16 = jnp.bfloat16

TILE = 256
GROUP = 16
HALF = 128
EPS = 1e-06
WINDOW = 21
PEERS = 2 * WINDOW


START = ([("a_start",)], [("b_start",)])
SERVE = {
    "stats": (
        [("a_near", "y"), ("a_near", "a")],
        [],
    ),
    "act0": (
        [("a_far", "y"), ("a_far", "a")],
        [("b_z", 1, 0), ("b_z", 1, 1)],
    ),
    "act1": (
        [],
        [("b_near", 0)],
    ),
    "pre00": (
        [("y_near", 0, 0), ("y_near", 0, 1), ("a_z", "y", 1, 0, 0), ("a_z", "y", 1, 1, 0), ("a_z", "y", 1, 0, 1), ("a_z", "y", 1, 1, 1), ("a_done", "y", 1), ("a_done", "y", -1), ("a_z", "a", 1, 0, 0), ("a_z", "a", 1, 1, 0), ("a_z", "a", 1, 0, 1), ("a_z", "a", 1, 1, 1), ("a_done", "a", 1), ("a_done", "a", -1), ("y_far", 0), ("a_z", "y", 2, 0, 0), ("a_z", "y", 2, 1, 0), ("y_near", 1, 0), ("y_near", 1, 1), ("a_z", "y", 2, 0, 1), ("a_z", "y", 2, 1, 1), ("a_done", "y", -2), ("a_done", "y", 2), ("a_z", "a", 2, 0, 0), ("a_z", "a", 2, 1, 0), ("y_near", -1, 0), ("y_near", -1, 1), ("a_z", "a", 2, 0, 1), ("a_z", "a", 2, 1, 1), ("a_done", "a", -2), ("a_done", "a", 2), ("a_z", "y", 3, 0, 0), ("a_z", "y", 3, 1, 0), ("y_far", 1), ("a_z", "y", 3, 0, 1), ("a_z", "y", 3, 1, 1), ("a_done", "y", 3), ("a_done", "y", -3)],
        [("b_z", 2, 0), ("b_z", 2, 1), ("b_near", -1), ("b_near", 1), ("b_far", 0), ("b_z", 3, 0), ("b_z", 3, 1), ("b_near", -2), ("b_near", 2), ("b_far", -1), ("b_far", 1), ("b_last",)],
    ),
    "post000": (
        [("a_z", "a", 3, 0, 0), ("a_z", "a", 3, 1, 0)],
        [],
    ),
    "post001": (
        [("y_near", -2, 0), ("y_near", -2, 1), ("a_z", "a", 3, 0, 1), ("a_z", "a", 3, 1, 1), ("a_done", "a", 3), ("a_done", "a", -3)],
        [("b_near", 3), ("b_near", -3)],
    ),
    "post002": (
        [],
        [("b_far", -2), ("b_far", 2)],
    ),
    "post010": (
        [("y_near", 2, 0), ("y_near", 2, 1), ("a_z", "y", 4, 0, 0)],
        [],
    ),
    "post011": (
        [("y_far", -1), ("a_z", "y", 4, 0, 1), ("a_done", "y", 4)],
        [("b_near", 4)],
    ),
    "post012": (
        [("a_z", "a", 4, 0, 0)],
        [],
    ),
    "post100": (
        [("y_near", 3, 0), ("y_near", 3, 1), ("a_z", "a", 4, 0, 1), ("a_done", "a", 4)],
        [("b_far", 3), ("b_far", -3)],
    ),
    "post102": (
        [("y_near", -3, 0), ("y_near", -3, 1)],
        [],
    ),
    "pre11": (
        [("y_far", -2), ("y_far", 2)],
        [("b_far", 4)],
    ),
    "post110": (
        [("y_near", 4, 0), ("y_near", 4, 1)],
        [],
    ),
    "post111": (
        [("y_far", 3)],
        [],
    ),
    "post112": (
        [("y_far", -3)],
        [],
    ),
    "post202": (
        [("y_far", 4)],
        [],
    ),
}


def lane_iota(shape):
    return lax.broadcasted_iota(jnp.int32, shape, len(shape) - 1)


def butterfly(values, step):
    lanes = lane_iota(values.shape)
    up = pltpu.roll(values, step, 1)
    down = pltpu.roll(values, HALF - step, 1)
    return values + jnp.where((lanes & step) != 0, up, down)


def fold_lanes(rows):
    return jnp.concatenate([rows[:, HALF * b : HALF * (b + 1)] for b in range(4)], axis=0)


def unfold_lanes(folded):
    return jnp.concatenate([folded[8 * b : 8 * (b + 1)] for b in range(4)], axis=1)


def group_sum(rows):
    folded = fold_lanes(rows)
    for step in (1, 2, 4, 8):
        folded = butterfly(folded, step)
    return folded


def pack_groups(folded):
    lanes = lane_iota((8, HALF))
    packed = jnp.zeros((8, HALF), F32)
    for b in range(4):
        packed = jnp.where((lanes & 3) == b, folded[8 * b : 8 * (b + 1)], packed)
    return packed


def unpack_groups(packed):
    lanes = lane_iota((8, HALF))
    blocks = []
    for b in range(4):
        block = jnp.where((lanes & 3) == b, packed, 0.0)
        block = butterfly(butterfly(block, 1), 2)
        blocks.append(block)
    return jnp.concatenate(blocks, axis=1)


def rows_of(parts):
    zeros = jnp.zeros((8 - len(parts), parts[0].shape[1]), F32)
    return jnp.concatenate(parts + [zeros], axis=0)


def tile_stats(ref):
    sums = rows_of(
        [jnp.sum(ref[TILE * j : TILE * (j + 1), :], axis=0, keepdims=True) for j in range(3)]
    )
    total = group_sum(sums)
    means = unfold_lanes(total * (1.0 / (TILE * GROUP)))
    seconds = []
    for j in range(3):
        off = ref[TILE * j : TILE * (j + 1), :] - means[j : j + 1]
        seconds.append(jnp.sum(off * off, axis=0, keepdims=True))
    spread = group_sum(rows_of(seconds))
    return pack_groups(total) + pltpu.roll(pack_groups(spread), 4, 0)


def image_stats(win, stat, me, starts, ends):
    rows = win.shape[0] + 8
    table = jnp.concatenate([win[...], stat[...]], axis=0)
    row = lax.broadcasted_iota(jnp.int32, (rows, HALF), 0)
    slot = row >> 3
    tile_row = row & 7
    offset = jnp.where(slot >= WINDOW, slot - WINDOW + 1, slot - WINDOW)
    offset = jnp.where(slot >= PEERS, 0, offset)
    tile = 3 * (me + offset) + tile_row
    second = pltpu.roll(table.reshape(rows // 8, 8, HALF), 4, 1).reshape(rows, HALF)
    tile_mean = table * (1.0 / (TILE * GROUP))
    means, inverses = [], []
    for j in range(3):
        member = (tile >= starts[j]) & (tile < ends[j]) & (tile_row < 3)
        count = jnp.full((1, HALF), (ends[j] - starts[j]) * (TILE * GROUP), jnp.int32).astype(F32)
        mean = jnp.sum(jnp.where(member, table, 0.0), axis=0, keepdims=True) / count
        away = tile_mean - mean
        moment = second + (TILE * GROUP) * (away * away)
        spread = jnp.sum(jnp.where(member, moment, 0.0), axis=0, keepdims=True) / count
        means.append(mean)
        inverses.append(lax.rsqrt(spread + EPS))
    packed = rows_of(means) + pltpu.roll(rows_of(inverses), 4, 0)
    return unpack_groups(packed)


def kernel(
    counts,
    widths,
    latents,
    weight,
    bias,
    gain,
    shift,
    gain2,
    hidden,
    mean_out,
    scale_out,
    local,
    halo,
    taps_a,
    taps_b,
    taps_y,
    acts,
    total,
    w_high,
    w_low,
    coef,
    stat1,
    stat2,
    win1,
    win2,
    local_sem,
    halo_send,
    halo_recv,
    stat_send,
    stat_recv,
    send_sem,
    recv_sem,
):
    t = lax.axis_index("tiles")
    s = lax.axis_index("sub")
    me = t * 8 + s
    z, x = t // 4, t % 4
    y, core = s // 2, s % 2

    def at(index):
        p = lax.rem(index + 256, 256)
        return (p // 8, p % 8)

    right = {
        "z+": (lax.rem(z + 1, 8) * 4 + x, s),
        "z-": (lax.rem(z + 7, 8) * 4 + x, s),
        "x+": (z * 4 + lax.rem(x + 1, 4), s),
        "x-": (z * 4 + lax.rem(x + 3, 4), s),
        "x2": (z * 4 + lax.rem(x + 2, 4), s),
        "y+": (t, lax.rem(y + 1, 4) * 2 + core),
        "y-": (t, lax.rem(y + 3, 4) * 2 + core),
        "c": (t, s + 1 - 2 * core),
    }

    def z_row(dz):
        return lax.rem(z + dz + 8, 8) * 4

    def row_of(dz, dx):
        return z_row(dz) + lax.rem(x + dx + 4, 4)

    odd = z % 2

    def s_row(ds):
        return z_row((1 - 2 * odd) * ds)

    barrier = pltpu.get_barrier_semaphore()

    def greet(step, carry):
        for sign in (1, -1):
            pl.semaphore_signal(barrier, inc=1, device_id=at(me + sign * step), device_id_type=MESH)
        return carry

    for name in ("z+", "z-", "x+", "x-", "x2", "y+", "y-"):
        pl.semaphore_signal(barrier, inc=1, device_id=right[name], device_id_type=MESH)
    lax.fori_loop(1, WINDOW + 1, greet, 0)

    load = pltpu.make_async_copy(latents, local, local_sem.at[0])
    load.start()

    own_a = pltpu.make_async_copy(weight.at[pl.ds(0, 1)], taps_a.at[t], local_sem.at[1])
    own_b = pltpu.make_async_copy(weight.at[pl.ds(1, 4)], taps_b.at[t], local_sem.at[1])
    own_y = pltpu.make_async_copy(weight.at[5 + y], taps_y.at[y, t], local_sem.at[2])

    @pl.when(core == 0)
    def _():
        own_y.start()
        own_a.start()

    @pl.when(core == 1)
    def _():
        own_b.start()

    tiles = [3 * me + j for j in range(3)]
    starts = [me * 0] * 3
    ends = [me * 0] * 3
    width = [me * 0 + 32] * 3
    begin = me * 0

    def place(i, carry):
        begin, starts, ends, width = carry
        end = begin + counts[i]
        inside = [(tile >= begin) & (tile < end) for tile in tiles]
        starts = [jnp.where(hit, begin, old) for hit, old in zip(inside, starts)]
        ends = [jnp.where(hit, end, old) for hit, old in zip(inside, ends)]
        width = [jnp.where(hit, widths[i], old) for hit, old in zip(inside, width)]
        return end, starts, ends, width

    _, starts, ends, width = lax.fori_loop(
        0, counts.shape[0], place, (begin, starts, ends, width)
    )

    def piece(part):
        kind, taps, first, count = part
        if kind == "y":
            return taps_y.at[pl.ds(taps[0], taps[1]), pl.ds(first, count)]
        ref = taps_a if kind == "a" else taps_b
        return ref.at[pl.ds(first, count), pl.ds(taps[0], taps[1])]

    sent = {0: [], 1: []}

    def remote(part, way, send_index, recv_index):
        ref = piece(part)
        return pltpu.make_async_remote_copy(
            src_ref=ref,
            dst_ref=ref,
            send_sem=send_sem.at[send_index],
            recv_sem=recv_sem.at[recv_index],
            device_id=right[way],
            device_id_type=MESH,
        )

    def send(owner, part, way, recv):
        remote(part, way, len(sent[owner]), recv).start()
        sent[owner].append((part[0], part[1][1], part[3]))

    def arrived(part, recv):
        remote(part, "c", 0, recv).wait_recv()

    group_of = {0: 0, -1: 1, 1: 2, -2: 3, 2: 4, -3: 5, 3: 6, 4: 7}
    a_all, b_all = (0, 1), (0, 4)
    onward = ("z+", "z-")

    def a_part(kind, first, count):
        return (kind, (y, 1) if kind == "y" else a_all, first, count)

    def a_start():
        own_y.wait()
        own_a.wait()
        for k, kind in enumerate("ya"):
            send(0, a_part(kind, row_of(0, 0), 1), "x+", 3 * k)
            send(0, a_part(kind, row_of(0, 0), 1), "x-", 3 * k + 1)
            send(0, a_part(kind, row_of(0, 0), 1), "x2", 3 * k + 2)

    def a_near(kind):
        k = "ya".index(kind)
        for way in range(2):
            arrived(a_part(kind, row_of(0, 1 if way else -1), 1), 3 * k + way)

    def a_far(kind):
        k = "ya".index(kind)
        arrived(a_part(kind, row_of(0, 2), 1), 3 * k + 2)
        for h in range(2):
            for way in range(2):
                part = a_part(kind, z_row(0) + 2 * h, 2)
                send(0, part, onward[way], 6 + 14 * k + 6 * way + h)
        a_done(kind, 0)

    def a_done(kind, dz):
        g = group_of[dz]
        part = a_part(kind, s_row(dz), 4)
        if kind == "y":
            send(0, part, "y+", 34 + 4 * g)
            send(0, part, "y-", 34 + 4 * g + 1)
        else:
            send(0, part, "c", 56 + g)

    def a_z(kind, d, way, h):
        k = "ya".index(kind)
        base = 6 + 14 * k
        if d == 4:
            arrived(a_part(kind, z_row(4) + 2 * h, 2), base + 12 + h)
            return
        part = a_part(kind, z_row(d if way else -d) + 2 * h, 2)
        arrived(part, base + 6 * way + 2 * (d - 1) + h)
        if d < 3:
            send(0, part, onward[way], base + 6 * way + 2 * d + h)
        elif way == h:
            send(0, part, onward[way], base + 12 + h)

    def y_near(dz, way):
        g = group_of[dz]
        tap = lax.rem(y + (1 if way else 3), 4)
        arrived(("y", (tap, 1), s_row(dz), 4), 34 + 4 * g + way)
        send(0, ("y", (tap, 1), s_row(dz) + 2 * way, 2), "y-" if way else "y+", 34 + 4 * g + 2 + way)

    def y_far(dz):
        g = group_of[dz]
        tap = lax.rem(y + 2, 4)
        for way in range(2):
            arrived(("y", (tap, 1), s_row(dz) + 2 * way, 2), 34 + 4 * g + 2 + way)
        send(0, ("y", (0, 4), s_row(dz), 4), "c", 64 + g)

    def b_halves(g):
        return ((0, 2), (2, 2))

    def b_spread(dz):
        g = group_of[dz]
        if 0 < abs(dz) < 4:
            g = 2 * dz - odd if dz > 0 else -2 * dz - 1 + odd
        part = ("b", b_all, row_of(dz, 0), 1)
        send(1, part, "x+", 8 + 4 * g)
        send(1, part, "x-", 8 + 4 * g + 1)

    def b_start():
        own_b.wait()
        part = ("b", b_all, row_of(0, 0), 1)
        send(1, part, "z+", 0)
        send(1, part, "z-", 3)
        b_spread(0)

    def b_z(d, way):
        dz = d if way else -d
        part = ("b", b_all, row_of(dz, 0), 1)
        arrived(part, 3 * way + d - 1)
        if d < 3:
            send(1, part, onward[way], 3 * way + d)
        else:
            send(1, ("b", b_halves(0)[way], row_of(dz, 0), 1), onward[way], 6 + way)
        b_spread(dz)

    def b_last():
        for way in range(2):
            arrived(("b", b_halves(0)[way], row_of(4, 0), 1), 6 + way)
        b_spread(4)

    def b_near(dz):
        g = group_of[dz]
        for way in range(2):
            first = s_row(dz) + lax.rem(x + (1 if way else 3), 4)
            arrived(("b", b_all, first, 1), 8 + 4 * g + way)
            send(1, ("b", b_halves(g)[way], first, 1), "x-" if way else "x+", 8 + 4 * g + 2 + way)

    def b_far(dz):
        g = group_of[dz]
        for way in range(2):
            arrived(("b", b_halves(g)[way], s_row(dz) + lax.rem(x + 2, 4), 1), 8 + 4 * g + 2 + way)
        send(1, ("b", b_all, s_row(dz), 4), "c", 66 + g)

    steps = {
        step.__name__: step
        for step in (
            a_start, a_near, a_far, a_done, a_z, y_near, y_far, b_start, b_z, b_last, b_near, b_far
        )
    }

    def serve(lists):
        for owner in range(2):
            if lists[owner]:

                @pl.when(core == owner)
                def _(owner=owner):
                    for name, *values in lists[owner]:
                        steps[name](*values)

    def serve_at(slot):
        if slot in SERVE:
            serve(SERVE[slot])

    def pair_arrived(groups, shared):
        @pl.when(core == 0)
        def _():
            for dz in groups if shared else ():
                arrived(("b", b_all, s_row(dz), 4), 66 + group_of[dz])

        @pl.when(core == 1)
        def _():
            for dz in groups:
                if shared:
                    arrived(("a", a_all, s_row(dz), 4), 56 + group_of[dz])
                else:
                    arrived(("y", (0, 4), s_row(dz), 4), 64 + group_of[dz])

    load.wait()
    stat1[...] = tile_stats(local)
    for h in range(8):
        rows = pl.ds(96 * h, 96)
        total[rows, :] = jnp.broadcast_to(bias[...], (96, 512))

    pl.semaphore_wait(barrier, PEERS + 7)
    serve(START)
    up = pltpu.make_async_remote_copy(
        src_ref=latents.at[pl.ds(5 * HALF, HALF), :],
        dst_ref=halo.at[0],
        send_sem=halo_send.at[0],
        recv_sem=halo_recv.at[0],
        device_id=at(me + 1),
        device_id_type=MESH,
    )
    down = pltpu.make_async_remote_copy(
        src_ref=latents.at[pl.ds(0, HALF), :],
        dst_ref=halo.at[1],
        send_sem=halo_send.at[1],
        recv_sem=halo_recv.at[1],
        device_id=at(me - 1),
        device_id_type=MESH,
    )

    def share(stat, win, which):
        def one(step, carry):
            for slot, to in ((WINDOW - step, me + step), (WINDOW - 1 + step, me - step)):
                pltpu.make_async_remote_copy(
                    src_ref=stat,
                    dst_ref=win.at[pl.ds(pl.multiple_of(slot * 8, 8), 8), :],
                    send_sem=stat_send.at[which],
                    recv_sem=stat_recv.at[which],
                    device_id=at(to),
                    device_id_type=MESH,
                ).start()
            return carry

        lax.fori_loop(1, WINDOW + 1, one, 0)

    def collect(win, which):
        ref = win
        both = pltpu.make_async_remote_copy(
            src_ref=ref,
            dst_ref=ref,
            send_sem=stat_send.at[which],
            recv_sem=stat_recv.at[which],
            device_id=at(me + 1),
            device_id_type=MESH,
        )
        both.wait_send()
        both.wait_recv()

    share(stat1, win1, 0)
    up.start()
    down.start()
    serve_at("stats")
    collect(win1, 0)
    coef[...] = image_stats(win1, stat1, me, starts, ends)
    up.wait()
    down.wait()

    def act_block(source, j, wide, stores):
        row = lax.broadcasted_iota(jnp.int32, (HALF, HALF), 0)
        column = row & (wide - 1)
        has_left = column != 0
        has_right = column != wide - 1
        for b in range(4):
            lanes = pl.ds(HALF * b, HALF)
            mean = coef[pl.ds(j, 1), lanes]
            scale = coef[pl.ds(j + 4, 1), lanes] * gain[:, HALF * b : HALF * (b + 1)]
            value = (source(lanes) - mean) * scale + shift[:, HALF * b : HALF * (b + 1)]
            act = value / (1.0 + jnp.exp(-value))
            shifted = (
                jnp.where(has_left, pltpu.roll(act, 1, 0), 0.0),
                act,
                jnp.where(has_right, pltpu.roll(act, HALF - 1, 0), 0.0),
            )
            for dx in range(3):
                high = shifted[dx].astype(BF16)
                low = (shifted[dx] - high.astype(F32)).astype(BF16)
                for base, valid in stores:
                    rows = pl.ds(base, HALF)
                    if valid is None:
                        acts[dx, 0, rows, lanes] = high
                        acts[dx, 1, rows, lanes] = low
                    else:
                        keep = jnp.where(valid, 1.0, 0.0).astype(F32)
                        acts[dx, 0, rows, lanes] = (high.astype(F32) * keep).astype(BF16)
                        acts[dx, 1, rows, lanes] = (low.astype(F32) * keep).astype(BF16)

    act_block(lambda lanes: halo[0, :, lanes], 0, width[0], [(0, tiles[0] > starts[0])])
    serve_at("act0")
    act_block(lambda lanes: halo[1, :, lanes], 2, width[2], [(2 * 512 + 384, tiles[2] + 1 < ends[2])])
    serve_at("act1")
    for q in range(6):
        j, half = q // 2, q % 2
        stores = [(j * 512 + HALF + half * HALF, None)]
        if half == 0 and j > 0:
            stores.append(((j - 1) * 512 + 384, tiles[j] > starts[j]))
        if half == 1 and j < 2:
            stores.append(((j + 1) * 512, tiles[j + 1] > starts[j + 1]))
        act_block(lambda lanes, q=q: local[HALF * q : HALF * (q + 1), lanes], j, width[j], stores)
        serve_at(f"act{q + 2}")

    first = z // 2
    order = [
        first,
        lax.rem(first + 3 + 2 * odd, 4),
        lax.rem(first + 1 + 2 * odd, 4),
        lax.rem(first + 2, 4),
    ]
    groups = [(0, 1), (-1, -2), (2, 3), (-3, 4)]

    def split_weights(chunk, taps):
        def fixed(c):
            for tap in taps:
                if tap < 1:
                    value = taps_a[8 * c : 8 * c + 8, tap : tap + 1]
                elif tap < 5:
                    value = taps_b[8 * c : 8 * c + 8, tap - 1 : tap]
                else:
                    value = taps_y[tap - 5 : tap - 4, 8 * c : 8 * c + 8]
                value = value.reshape(HALF, 512)
                to = pl.ds(tap * HALF, HALF)
                high = value.astype(BF16)
                w_high[to, :] = high
                w_low[to, :] = (value - high.astype(F32)).astype(BF16)

        for c in range(4):
            pl.when(chunk == c)(functools.partial(fixed, c))

    def multiply(chunk, taps, j):
        lanes = pl.ds(pl.multiple_of(chunk * HALF, HALF), HALF)
        wide = width[j]
        is_wide, is_middle = wide == 128, wide == 64

        def columns(part):
            blocks = []
            for tap in taps:
                dy, dx = tap // 3 - 1, tap % 3
                base = j * 512 + HALF
                if dy == 0:
                    blocks.append(acts[dx, part, pl.ds(base, TILE), lanes])
                    continue
                near = acts[dx, part, pl.ds(base + 32 * dy, TILE), lanes]
                middle = acts[dx, part, pl.ds(base + 64 * dy, TILE), lanes]
                far = acts[dx, part, pl.ds(base + 128 * dy, TILE), lanes]
                blocks.append(jnp.where(is_wide, far, jnp.where(is_middle, middle, near)))
            return jnp.concatenate(blocks, axis=1)

        weight_rows = pl.ds(taps[0] * HALF, len(taps) * HALF)
        high = columns(0)
        low = columns(1)
        w1, w2 = w_high[weight_rows, :], w_low[weight_rows, :]
        out = jnp.dot(
            jnp.concatenate([high, low, high], axis=1),
            jnp.concatenate([w1, w1, w2], axis=0),
            preferred_element_type=F32,
        )
        rows = pl.ds(pl.multiple_of(j * TILE, TILE), TILE)
        total[rows, :] += out

    for k in range(4):
        for part, taps in enumerate((range(0, 5), range(5, 9))):
            serve_at(f"pre{k}{part}")
            pair_arrived(groups[k], part == 0)
            split_weights(order[k], taps)
            for j in range(3):
                multiply(order[k], taps, j)
                serve_at(f"post{k}{part}{j}")

    store = pltpu.make_async_copy(total, hidden, local_sem.at[6])
    store.start()
    stat2[...] = tile_stats(total)
    share(stat2, win2, 1)
    for owner in range(2):

        @pl.when(core == owner)
        def _(owner=owner):
            for index, (kind, taps, count) in enumerate(sent[owner]):
                remote((kind, (0, taps), 0, count), "c", index, 0).wait_send()

    collect(win2, 1)
    final = image_stats(win2, stat2, me, starts, ends)
    mean_out[...] = final[0:3]
    scale_out[...] = final[4:7] * gain2[...]
    store.wait()


def shards(latents, weight, bias, gain1, shift1, gain2, shift2, tile_counts, widths):
    vmem = pl.BlockSpec(memory_space=pltpu.VMEM)
    smem = pl.BlockSpec(memory_space=pltpu.SMEM)
    hbm = pl.BlockSpec(memory_space=pl.ANY)
    dma = pltpu.SemaphoreType.DMA
    pixels, channels = latents.shape
    hidden, mean, scale = pl.pallas_call(
        kernel,
        out_shape=(
            jax.ShapeDtypeStruct((pixels, channels), F32),
            jax.ShapeDtypeStruct((3, channels), F32),
            jax.ShapeDtypeStruct((3, channels), F32),
        ),
        in_specs=[smem, smem, hbm, hbm, vmem, vmem, vmem, vmem],
        out_specs=(hbm, vmem, vmem),
        scratch_shapes=[
            pltpu.VMEM((pixels, channels), F32),
            pltpu.VMEM((2, HALF, channels), F32),
            pltpu.VMEM((32, 1, 16, channels), F32),
            pltpu.VMEM((32, 4, 16, channels), F32),
            pltpu.VMEM((4, 32, 16, channels), F32),
            pltpu.VMEM((3, 2, 1536, channels), BF16),
            pltpu.VMEM((pixels, channels), F32),
            pltpu.VMEM((9 * HALF, channels), BF16),
            pltpu.VMEM((9 * HALF, channels), BF16),
            pltpu.VMEM((8, channels), F32),
            pltpu.VMEM((8, HALF), F32),
            pltpu.VMEM((8, HALF), F32),
            pltpu.VMEM((8 * PEERS, HALF), F32),
            pltpu.VMEM((8 * PEERS, HALF), F32),
            dma((7,)),
            dma((2,)),
            dma((2,)),
            dma((2,)),
            dma((2,)),
            dma((96,)),
            dma((80,)),
        ],
        compiler_params=pltpu.CompilerParams(
            collective_id=0, has_side_effects=True, vmem_limit_bytes=60 << 20
        ),
        name="block",
    )(
        tile_counts,
        widths,
        latents,
        jnp.transpose(weight, (1, 0, 2)),
        bias.reshape(1, -1),
        gain1.reshape(1, -1),
        shift1.reshape(1, -1),
        gain2.reshape(1, -1),
    )
    centred = hidden.reshape(3, TILE, channels) - mean[:, None, :]
    value = centred * scale[:, None, :] + shift2
    return jax.nn.silu(value).reshape(pixels, channels)


def solution(mesh):
    return jax.shard_map(
        shards,
        mesh=mesh,
        in_specs=(
            P(("tiles", "sub"), None),
            P("tiles", None, None),
            P(),
            P(),
            P(),
            P(),
            P(),
            P(),
            P(),
        ),
        out_specs=P(("tiles", "sub"), None),
        check_vma=False,
    )
```
